128 devices in a mesh: dp: 16 (over z, y_lo, core), fsdp: 8 (over y_hi, x).
Axes of the slice: x: 4, y: 4 (y_hi: 2, y_lo: 2; y = y_hi * 2 + y_lo), z: 4, core: 2. Of those that a mesh axis runs over, the one named last changes fastest.
Arguments:
- queries: bfloat16 [49152, 2048], P(('dp', 'fsdp')), may hold values from -210 to 210
- enc_store: bfloat16 [2048, 128, 512], P(('dp', 'fsdp')), may hold values from -6 to 6
- kv_weight: bfloat16 [512, 2, 2048], P('fsdp'), may hold values from -0.25 to 0.25
- table: int32 [768, 2], replicated, may hold values from 0 to 2047, as said below
- cotangent: bfloat16 [49152, 2048], P(('dp', 'fsdp')), may hold values from -6 to 6
Outputs:
- attended: bfloat16 [49152, 2048], P(('dp', 'fsdp'))
- d_queries: bfloat16 [49152, 2048], P(('dp', 'fsdp'))
- d_store: bfloat16 [2048, 128, 512], P(('dp', 'fsdp'))
- grad_kv: float32 [512, 2, 2048], P('fsdp')
The draws below stay inside these ranges and needn't reach their ends.
Inputs may be any that keep to these rules, and one draw needn't show every extreme that they name: `table`: the windows of device (d, f) (rows of the arrays in the order dp then fsdp) name only encodings stored on devices (d', f) with the same fsdp index. The 12 encodings named by one device's windows come from exactly 6 encoder devices, 2 from each. An encoding may be named more than once.
All inputs are finite; a program needn't handle non-finite values.
Results may differ from the reference program's by a relative error of at most 0.015.
The reference program's roundings to bfloat16 on the way count: a program that leaves them out, or rounds other values in their place, can miss the bound.
Values may be sent and summed in bfloat16 or wider, within the bound.
A program may use at most 192 MiB of HBM per device.

```python
import jax
import jax.numpy as jnp
from jax import lax

HEAD = 128
ENC = 512
WIN = 64
BLOCK = 128
NEIGH = 2
CAP = 2
WIN_DEV = 6
BLK_DEV = 16
HQ = 2048
WINDOWS = 768
TOKENS = 49152
BLOCKS = 2048
NROWS = 196608
N_DP = 16
N_FSDP = 8


def draw_table(key, part):
    n_req = WIN_DEV * NEIGH
    n_src = n_req // CAP

    def one_device(device):
        dev_key = jax.random.fold_in(key, device)
        key_src, key_mix, key_blk = jax.random.split(dev_key, 3)
        chosen = jax.random.permutation(key_src, N_DP)[:n_src]
        sources = jnp.repeat(chosen, CAP)
        sources = jax.random.permutation(key_mix, sources)
        local_blk = jax.random.randint(key_blk, (n_req,), 0, BLK_DEV)
        column = device % N_FSDP
        return (sources * N_FSDP + column) * BLK_DEV + local_blk
    devices = jnp.arange(N_DP * N_FSDP)
    return jax.vmap(one_device)(devices).reshape(WINDOWS, NEIGH).astype(jnp.int32)


def draw_queries(key, part):
    key_base = jax.random.fold_in(key, 7)
    values = jnp.clip(jax.random.normal(key_base, (TOKENS, HQ), jnp.float32), -6.0, 6.0)
    return values.astype(jnp.bfloat16)


def draw_cotangent(key, part):
    key_base = jax.random.fold_in(key, 13)
    values = jnp.clip(jax.random.normal(key_base, (TOKENS, HQ), jnp.float32), -6.0, 6.0)
    return values.astype(jnp.bfloat16)


def block_levels(own_key, dims, shards, low, high):
    level = 1.0
    for dim, blocks in shards:
        heights = jax.random.uniform(jax.random.fold_in(jax.random.fold_in(own_key, 6), dim), (blocks,), jnp.float32, low / len(shards), high / len(shards))
        level = level * jnp.repeat(jnp.exp(heights), dims[dim] // blocks).reshape((-1,) + (1,) * (len(dims) - 1 - dim))
    return level


def normal_values(stream_key, extent, spread, limit, pieces=(), kind=jnp.bfloat16):
    entries = jax.random.normal(stream_key, extent, jnp.float32) * spread
    if len(pieces) > 0:
        entries = block_levels(stream_key, extent, pieces, -0.22, 0.18) * entries
    return jnp.clip(entries, min=-limit, max=limit).astype(kind)


def setup_inputs(seed: int = 0) -> dict:
    key_list = jax.random.split(jax.random.key(seed), 6)
    return {
        "queries": draw_queries(jax.random.fold_in(key_list[5], 71), 0),
        "enc_store": normal_values(key_list[1], (BLOCKS, BLOCK, ENC), 1.0, 6.0, ((0, 128),)),
        "kv_weight": normal_values(key_list[2], (ENC, 2, HQ), ENC ** -0.5, 0.25, ((0, 8),)),
        "table": draw_table(jax.random.fold_in(key_list[5], 71), 0),
        "cotangent": draw_cotangent(jax.random.fold_in(key_list[5], 71), 0),
    }


def window_pass(query_win, neighbours, weight_flat, cot_win):
    count = query_win.shape[0]
    hq_width = weight_flat.shape[1] // 2
    heads = hq_width // HEAD
    scale = HEAD ** -0.5
    enc_flat = neighbours.reshape(-1, neighbours.shape[-1])
    kv_proj = jnp.dot(enc_flat, weight_flat, preferred_element_type=jnp.float32).astype(jnp.bfloat16)
    kv_proj = kv_proj.reshape(count, NEIGH * BLOCK, 2, heads, HEAD)
    keys = kv_proj[:, :, 0].astype(jnp.float32)
    values = kv_proj[:, :, 1].astype(jnp.float32)
    query_heads = query_win.reshape(count, WIN, heads, HEAD).astype(jnp.float32)
    cot_heads = cot_win.reshape(count, WIN, heads, HEAD).astype(jnp.float32)
    scores = jnp.einsum("gqhd,gkhd->ghqk", query_heads, keys) * scale
    top = jnp.max(scores, axis=-1, keepdims=True)
    expo = jnp.exp(scores - top)
    probs = expo / jnp.sum(expo, axis=-1, keepdims=True)
    probs_b = probs.astype(jnp.bfloat16).astype(jnp.float32)
    attended = jnp.einsum("ghqk,gkhd->gqhd", probs_b, values).astype(jnp.bfloat16)
    d_probs = jnp.einsum("gqhd,gkhd->ghqk", cot_heads, values)
    d_values = jnp.einsum("ghqk,gqhd->gkhd", probs_b, cot_heads)
    d_scores = probs * (d_probs - jnp.sum(d_probs * probs, axis=-1, keepdims=True)) * scale
    d_scores = d_scores.astype(jnp.bfloat16).astype(jnp.float32)
    d_query = jnp.einsum("ghqk,gkhd->gqhd", d_scores, keys).astype(jnp.bfloat16)
    d_keys = jnp.einsum("ghqk,gqhd->gkhd", d_scores, query_heads)
    d_kv = jnp.stack([d_keys, d_values], axis=2).astype(jnp.bfloat16).reshape(-1, 2 * hq_width)
    d_neigh = jnp.dot(d_kv, weight_flat.T, preferred_element_type=jnp.float32).astype(jnp.bfloat16)
    grad_part = jnp.dot(enc_flat.T, d_kv, preferred_element_type=jnp.float32)
    return attended.reshape(count, WIN, hq_width), d_query.reshape(count, WIN, hq_width), d_neigh, grad_part


def reference(queries, enc_store, kv_weight, table, cotangent):
    group = WIN_DEV * N_FSDP
    n_groups = WINDOWS // group
    weight_flat = kv_weight.reshape(ENC, 2 * HQ)
    query_groups = queries.reshape(n_groups, group, WIN, HQ)
    table_groups = table.reshape(n_groups, group, NEIGH)
    cot_groups = cotangent.reshape(n_groups, group, WIN, HQ)

    def step(carry, inputs):
        query_win, table_win, cot_win = inputs
        neighbours = enc_store[table_win].reshape(group, NEIGH * BLOCK, ENC)
        attended, d_query, d_neigh, grad_part = window_pass(query_win, neighbours, weight_flat, cot_win)
        return carry + grad_part, (attended, d_query, d_neigh)

    start_grad = jnp.zeros((ENC, 2 * HQ), jnp.float32)
    grad_sum, stacked = lax.scan(step, start_grad, (query_groups, table_groups, cot_groups))
    attended = stacked[0].reshape(TOKENS, HQ)
    d_queries = stacked[1].reshape(TOKENS, HQ)
    d_pieces = stacked[2].reshape(WINDOWS * NEIGH, BLOCK * ENC).astype(jnp.float32)
    d_store = jnp.zeros((BLOCKS, BLOCK * ENC), jnp.float32).at[table.reshape(-1)].add(d_pieces)
    d_store = d_store.astype(jnp.bfloat16).reshape(BLOCKS, BLOCK, ENC)
    grad_kv = (grad_sum * (NROWS ** -0.5)).reshape(ENC, 2, HQ)
    return attended, d_queries, d_store, grad_kv
```

```python
import jax
import jax.numpy as jnp
from jax import lax
from jax.experimental import pallas as pl
from jax.experimental.pallas import tpu as pltpu
from jax.sharding import PartitionSpec as P

HEAD = 128
WIN = 64
BLOCK = 128
NEIGH = 2
CAP = 2
NZ, NY, NC = 4, 2, 2
NYH, NX = 2, 4
N_DP, N_FSDP = NZ * NY * NC, NYH * NX
PHASES = 4
ROWS = BLOCK // PHASES
SCALE = HEAD ** (-0.5)
MESH = pl.DeviceIdType.MESH
f32, bf16 = jnp.float32, jnp.bfloat16
ORDER = (
    (2, 1, 0), (2, 1, 1), (2, 0, 0), (2, 0, 1),
    (1, 1, 0), (3, 1, 0), (1, 1, 1), (3, 1, 1),
    (1, 0, 0), (3, 0, 0), (1, 0, 1), (3, 0, 1),
    (0, 1, 0), (0, 1, 1), (0, 0, 1),
)
GRAD_TILE = 512


def mm(a, b):
    return jnp.dot(a, b, preferred_element_type=f32)


def mm_nt(a, b):
    return lax.dot_general(a, b, (((1,), (1,)), ((), ())), preferred_element_type=f32)


def mm_tn(a, b):
    return lax.dot_general(a, b, (((0,), (0,)), ((), ())), preferred_element_type=f32)


def place():
    dp = lax.axis_index("dp")
    fs = lax.axis_index("fsdp")
    return dp, fs, dp // (NY * NC), (dp // NC) % NY, dp % NC, fs // NX, fs % NX


def two_heads(rows):
    lane = lax.broadcasted_iota(jnp.int32, rows.shape, 1)
    zero = jnp.zeros_like(rows)
    return jnp.concatenate([jnp.where(lane < HEAD, rows, zero), jnp.where(lane < HEAD, zero, rows)], axis=0)


def own_halves(full):
    return jnp.concatenate([full[:WIN, :HEAD], full[WIN:, HEAD:]], axis=1)


def pair_first(loaded):
    query, cot, keys, values = loaded
    query2, cot2 = two_heads(query), two_heads(cot)
    return query2, cot2, mm_nt(keys, query2), mm_nt(values, cot2)


def pair_softmax(first):
    query2, cot2, scores, d_probs = first
    expo = jnp.exp((scores - jnp.max(scores, axis=0, keepdims=True)) * SCALE)
    probs = expo * (1.0 / jnp.sum(expo, axis=0, keepdims=True))
    inner = jnp.sum(d_probs * probs, axis=0, keepdims=True)
    d_scores = ((probs * SCALE) * (d_probs - inner)).astype(bf16)
    return query2, cot2, probs.astype(bf16), d_scores


def pair_last(second, loaded):
    query2, cot2, probs_b, d_scores = second
    _, _, keys, values = loaded
    return (
        own_halves(mm_tn(probs_b, values)).astype(bf16),
        own_halves(mm_tn(d_scores, keys)).astype(bf16),
        mm(d_scores, query2).astype(bf16),
        mm(probs_b, cot2).astype(bf16),
    )


def attend(win, q_ref, c_ref, kv_ref, att_ref, dq_ref):
    width = q_ref.shape[1]
    pairs = width // (2 * HEAD)
    row = pl.ds(pl.multiple_of(win * WIN, WIN), WIN)
    blk = pl.ds(win * NEIGH, NEIGH)
    keys_of = NEIGH * BLOCK

    def cols(pair, base):
        return pl.ds(base + pair * 2 * HEAD, 2 * HEAD)

    loaded = [
        (
            q_ref[row, cols(i, 0)],
            c_ref[row, cols(i, 0)],
            kv_ref[blk, :, cols(i, 0)].reshape(keys_of, 2 * HEAD),
            kv_ref[blk, :, cols(i, width)].reshape(keys_of, 2 * HEAD),
        )
        for i in range(pairs)
    ]
    ahead = 2
    first = [pair_first(loaded[i]) for i in range(min(ahead, pairs))]
    second, last = [], []
    for i in range(pairs):
        second.append(pair_softmax(first[i]))
        if i + ahead < pairs:
            first.append(pair_first(loaded[i + ahead]))
        if i >= 1:
            last.append(pair_last(second[i - 1], loaded[i - 1]))
    last.append(pair_last(second[-1], loaded[-1]))
    for i, (att, d_query, d_key, d_value) in enumerate(last):
        att_ref[row, cols(i, 0)] = att
        dq_ref[row, cols(i, 0)] = d_query
        kv_ref[blk, :, cols(i, 0)] = d_key.reshape(NEIGH, BLOCK, 2 * HEAD)
        kv_ref[blk, :, cols(i, width)] = d_value.reshape(NEIGH, BLOCK, 2 * HEAD)


def first_two(table_ref, base, n_req, source, value_of):
    first, second, count = jnp.int32(0), jnp.int32(0), jnp.int32(0)
    for r in range(n_req):
        entry = table_ref[base + r]
        hit = value_of.source(entry) == source
        value = value_of.value(entry, r)
        first = jnp.where(hit & (count == 0), value, first)
        second = jnp.where(hit & (count == 1), value, second)
        count = count + hit.astype(jnp.int32)
    return first, second, count


class Local:
    def __init__(self, blk_dev):
        self.blk_dev = blk_dev

    def source(self, entry):
        return entry // (self.blk_dev * N_FSDP)

    def value(self, entry, r):
        return entry % self.blk_dev


class Request(Local):
    def value(self, entry, r):
        return jnp.int32(r)


def main_kernel(
    table_ref, q_hbm, store_hbm, w_hbm, c_hbm,
    att_hbm, dq_hbm, back_hbm, grad_hbm,
    q_ref, c_ref, store_ref, w_ref, send_ref, recv0, recv1, recv2, recv3,
    kv_ref, enc_ref, enc_t_ref, att_ref, dq_ref, dn_ref,
    gs_ref, go_ref, gr_ref, rs_ref, ds_ref, dr_ref, ag_ref,
    pick_ref, slot_ref, inv_ref,
    in_sem, out_sem, a_send, a_recv, w_send, w_recv, ws_send, ws_recv,
    b_send, b_recv, g_send, g_recv, r_send, r_recv, d_send, d_recv, o_send, o_recv,
):
    recvs = (recv0, recv1, recv2, recv3)
    dp, fs, z, yl, core, yh, x = place()
    blk_dev = store_ref.shape[0]
    n_req = kv_ref.shape[0]
    hq = q_ref.shape[1]
    enc_width = store_ref.shape[2]
    w_rows = w_hbm.shape[0]
    w_half = w_rows // NC
    sib = (core + 1) % NC

    def dp_dev(dz, dy, dc):
        return (((z + dz) % NZ) * (NY * NC) + ((yl + dy) % NY) * NC + (core + dc) % NC, fs)

    def fs_dev(dyh, dx):
        ylo = (yl + dyh) % NY
        return (z * (NY * NC) + ylo * NC + core, ((yh + dyh) % NYH) * NX + (x + dx) % NX)

    FS = [(dyh, dx) for dyh in range(NYH) for dx in range(NX) if (dyh, dx) != (0, 0)]

    def remote(src, dst, ssem, rsem, dev):
        return pltpu.make_async_remote_copy(
            src_ref=src, dst_ref=dst, send_sem=ssem, recv_sem=rsem, device_id=dev, device_id_type=MESH
        )

    own_w = w_ref.at[fs]
    loads = [
        pltpu.make_async_copy(store_hbm, store_ref, in_sem.at[0]),
        pltpu.make_async_copy(w_hbm.at[pl.ds(0, w_half)], own_w.at[0], in_sem.at[1]),
        pltpu.make_async_copy(w_hbm.at[pl.ds(w_half, w_half)], own_w.at[1], in_sem.at[2]),
        pltpu.make_async_copy(q_hbm, q_ref, in_sem.at[3]),
        pltpu.make_async_copy(c_hbm, c_ref, in_sem.at[4]),
    ]
    for copy in loads:
        copy.start()
    barrier = pltpu.get_barrier_semaphore()
    partners = [dp_dev(*o) for o in ORDER] + [fs_dev(*o) for o in FS]
    for dev in partners:
        pl.semaphore_signal(barrier, inc=1, device_id=dev, device_id_type=MESH)

    def picks(i, carry):
        dst = ((z + i // 4) % NZ) * (NY * NC) + ((yl + (i // 2) % 2) % NY) * NC + (core + i % 2) % NC
        base = (dst * N_FSDP + fs) * n_req
        a, b, _ = first_two(table_ref, base, n_req, dp, Local(blk_dev))
        pick_ref[2 * i] = a
        pick_ref[2 * i + 1] = b
        return carry

    lax.fori_loop(0, N_DP, picks, 0)
    loads[1].wait()
    loads[2].wait()
    loads[0].wait()
    pl.semaphore_wait(barrier, len(partners))

    w_copies = []
    for j, (dyh, dx) in enumerate(FS):
        part = w_ref.at[fs, core]
        copy = remote(part, part, w_send.at[j], w_recv.at[j], fs_dev(dyh, dx))
        copy.start()
        w_copies.append(copy)

    a_copies = []
    for p in range(PHASES):
        rows = pl.ds(p * ROWS, ROWS)
        for dz, dy, dc in ORDER:
            i = dz * 4 + dy * 2 + dc
            for k in range(CAP):
                send_ref[p, 2 * i + k] = store_ref[pick_ref[2 * i + k], rows, :]
            slot = pl.ds(2 * i, CAP)
            copy = remote(send_ref.at[p, slot], recvs[p].at[slot], a_send.at[p, i], a_recv.at[p, i], dp_dev(dz, dy, dc))
            copy.start()
            a_copies.append(copy)
        for k in range(CAP):
            recvs[p][k] = store_ref[pick_ref[k], rows, :]

    mine = (dp * N_FSDP + fs) * n_req

    def slots(i, carry):
        src = ((z + NZ - i // 4) % NZ) * (NY * NC) + ((yl + (i // 2) % 2) % NY) * NC + (core + i % 2) % NC
        a, b, _ = first_two(table_ref, mine, n_req, src, Request(blk_dev))
        inv_ref[2 * i] = a
        inv_ref[2 * i + 1] = b
        return carry

    lax.fori_loop(0, N_DP, slots, 0)
    sources = [table_ref[mine + r] // (blk_dev * N_FSDP) for r in range(n_req)]
    for r in range(n_req):
        s = sources[r]
        dz = (z + NZ - s // (NY * NC)) % NZ
        index = dz * 4 + ((yl + (s // NC) % NY) % NY) * 2 + (core + s % NC) % NC
        seen = jnp.int32(0)
        for earlier in range(r):
            seen = seen + (sources[earlier] == s).astype(jnp.int32)
        slot_ref[r] = index * 2 + jnp.minimum(seen, CAP - 1)

    ws_copies = []
    for j, (dyh, dx) in enumerate(FS):
        w_copies[j].wait_recv()
        src_fs = ((yh + dyh) % NYH) * NX + (x + NX - dx) % NX
        part = w_ref.at[src_fs, core]
        copy = remote(part, part, ws_send.at[j], ws_recv.at[j], dp_dev(0, 0, 1))
        copy.start()
        ws_copies.append(copy)
    for copy in ws_copies:
        copy.wait_recv()

    for p in range(PHASES):
        for copy in a_copies[p * len(ORDER):(p + 1) * len(ORDER)]:
            copy.wait_recv()
        rows = pl.ds(p * ROWS, ROWS)
        for r in range(n_req):
            enc_ref[p, r] = recvs[p][slot_ref[r]]

        @pl.loop(0, kv_ref.shape[2] // 1024)
        def _(t):
            c = pl.ds(pl.multiple_of(t * 1024, 1024), 1024)
            out = mm(enc_ref[p].reshape(n_req * ROWS, enc_width), w_ref[:, :, :, c].reshape(enc_width, 1024))
            kv_ref[:, rows, c] = out.astype(bf16).reshape(n_req, ROWS, 1024)

    loads[3].wait()
    loads[4].wait()

    @pl.loop(0, n_req // NEIGH)
    def _(win):
        attend(win, q_ref, c_ref, kv_ref, att_ref, dq_ref)

    outs = [
        pltpu.make_async_copy(att_ref, att_hbm, out_sem.at[0]),
        pltpu.make_async_copy(dq_ref, dq_hbm, out_sem.at[1]),
    ]
    for copy in outs:
        copy.start()
    for copy in a_copies:
        copy.wait_send()

    b_copies = []
    for p in range(PHASES):
        rows = pl.ds(p * ROWS, ROWS)
        lhs = kv_ref[:, rows, :].reshape(n_req * ROWS, 2 * hq)

        @pl.loop(0, 2)
        def _(t):
            part = w_ref[pl.ds(t * (N_FSDP // 2), N_FSDP // 2)].reshape(enc_width // 2, 2 * hq)
            c = pl.ds(pl.multiple_of(t * (enc_width // 2), enc_width // 2), enc_width // 2)
            dn_ref[:, :, c] = mm_nt(lhs, part).astype(bf16).reshape(n_req, ROWS, enc_width // 2)

        for dz, dy, dc in ORDER + ((0, 0, 0),):
            i = dz * 4 + dy * 2 + dc
            for k in range(CAP):
                send_ref[p, 2 * i + k] = dn_ref[inv_ref[2 * i + k]]
            slot = pl.ds(2 * i, CAP)
            if i == 0:
                copy = pltpu.make_async_copy(send_ref.at[p, slot], back_hbm.at[p, slot], out_sem.at[2 + p])
                outs.append(copy)
            else:
                copy = remote(
                    send_ref.at[p, slot], back_hbm.at[p, slot], b_send.at[p, i], b_recv.at[p, i],
                    dp_dev((NZ - dz) % NZ, dy, dc),
                )
                b_copies.append(copy)
            copy.start()

    enc_rows = jnp.concatenate([enc_ref[p] for p in range(PHASES)], axis=1).reshape(n_req * BLOCK, enc_width)
    enc_t_ref[...] = enc_rows.T

    def grad_tile(half, t):
        c = pl.ds(pl.multiple_of(half * hq + t * GRAD_TILE, GRAD_TILE), GRAD_TILE)
        return mm(enc_t_ref[...], kv_ref[:, :, c].reshape(n_req * BLOCK, GRAD_TILE)).reshape(
            N_FSDP, w_rows, GRAD_TILE
        )

    n_tiles = hq // GRAD_TILE
    g_copies = []
    for t in range(n_tiles):
        gs_ref[t] = grad_tile(sib, t).astype(bf16)
        copy = remote(gs_ref.at[t], gr_ref.at[t], g_send.at[t], g_recv.at[t], dp_dev(0, 0, 1))
        copy.start()
        g_copies.append(copy)
    for t in range(n_tiles):
        go_ref[t] = grad_tile(core, t)
    r_copies = []
    for t in range(n_tiles):
        g_copies[t].wait()
        both = go_ref[t] + gr_ref[t].astype(f32)
        gs_ref[t] = both.astype(bf16)
        for j, (dyh, dx) in enumerate(FS):
            dst_fs = ((yh + dyh) % NYH) * NX + (x + dx) % NX
            copy = remote(gs_ref.at[t, dst_fs], rs_ref.at[t, j], r_send.at[t, j], r_recv.at[t, j], fs_dev(dyh, dx))
            copy.start()
            r_copies.append(copy)
    part_cols = hq // (NZ * NY)
    per_tile = GRAD_TILE // part_cols
    for t in range(n_tiles):
        for copy in r_copies[t * len(FS):(t + 1) * len(FS)]:
            copy.wait_recv()
        total = gs_ref[t, fs].astype(f32)
        for j in range(len(FS)):
            total = total + rs_ref[t, j].astype(f32)
        for s in range(per_tile):
            ds_ref[t * per_tile + s] = total[:, s * part_cols:(s + 1) * part_cols].astype(bf16)
    chips = [(dz, dy) for dz in range(NZ) for dy in range(NY) if (dz, dy) != (0, 0)]
    d_copies = []
    for m, (dz, dy) in enumerate(chips):
        chip = ((z + dz) % NZ) * NY + (yl + dy) % NY
        copy = remote(ds_ref.at[chip], dr_ref.at[m], d_send.at[m], d_recv.at[m], dp_dev(dz, dy, 0))
        copy.start()
        d_copies.append(copy)
    own_chip = z * NY + yl
    total = ds_ref[own_chip].astype(f32)
    for m in range(len(chips)):
        d_copies[m].wait_recv()
        total = total + dr_ref[m].astype(f32)
    ag_ref[...] = total.astype(bf16)
    piece = grad_hbm.at[core * (NZ * NY) + own_chip]
    copy = pltpu.make_async_copy(ag_ref, piece, out_sem.at[2 + PHASES])
    copy.start()
    outs.append(copy)
    o_copies = []
    for dz, dy, dc in ORDER:
        i = dz * 4 + dy * 2 + dc
        copy = remote(ag_ref, piece, o_send.at[i], o_recv.at[i], dp_dev(dz, dy, dc))
        copy.start()
        o_copies.append(copy)
    for copy in outs:
        copy.wait()
    for copy in w_copies + ws_copies + r_copies + d_copies:
        copy.wait_send()
    for copy in b_copies + o_copies:
        copy.wait()


def main_call(table, queries, enc_store, weight, cotangent):
    tokens, hq = queries.shape
    blk_dev, _, enc_width = enc_store.shape
    n_req = tokens // WIN * NEIGH
    w_rows = weight.shape[0]
    n_slots = N_DP * CAP
    n_tiles = hq // GRAD_TILE
    n_chips = NZ * NY
    hbm = pl.BlockSpec(memory_space=pl.ANY)
    vm = pltpu.VMEM
    sem = pltpu.SemaphoreType.DMA
    recv = vm((n_slots, ROWS, enc_width), bf16)
    scratch = [
        vm((tokens, hq), bf16), vm((tokens, hq), bf16), vm(enc_store.shape, bf16),
        vm((N_FSDP, NC, w_rows // NC, 2 * hq), bf16), vm((PHASES, n_slots, ROWS, enc_width), bf16),
        recv, recv, recv, recv,
        vm((n_req, BLOCK, 2 * hq), bf16), vm((PHASES, n_req, ROWS, enc_width), bf16),
        vm((enc_width, n_req * BLOCK), bf16), vm((tokens, hq), bf16), vm((tokens, hq), bf16),
        vm((n_req, ROWS, enc_width), bf16),
        vm((n_tiles, N_FSDP, w_rows, GRAD_TILE), bf16), vm((n_tiles, N_FSDP, w_rows, GRAD_TILE), f32),
        vm((n_tiles, N_FSDP, w_rows, GRAD_TILE), bf16), vm((n_tiles, N_FSDP - 1, w_rows, GRAD_TILE), bf16),
        vm((n_chips, w_rows, hq // n_chips), bf16), vm((n_chips - 1, w_rows, hq // n_chips), bf16),
        vm((w_rows, hq // n_chips), bf16),
        pltpu.SMEM((n_slots,), jnp.int32), pltpu.SMEM((n_req,), jnp.int32), pltpu.SMEM((n_slots,), jnp.int32),
        sem((5,)), sem((3 + PHASES,)), sem((PHASES, N_DP)), sem((PHASES, N_DP)),
        sem((N_FSDP - 1,)), sem((N_FSDP - 1,)), sem((N_FSDP - 1,)), sem((N_FSDP - 1,)),
        sem((PHASES, N_DP)), sem((PHASES, N_DP)), sem((n_tiles,)), sem((n_tiles,)),
        sem((n_tiles, N_FSDP - 1)), sem((n_tiles, N_FSDP - 1)), sem((n_chips - 1,)), sem((n_chips - 1,)),
        sem((N_DP,)), sem((N_DP,)),
    ]
    return pl.pallas_call(
        main_kernel,
        out_shape=[
            jax.ShapeDtypeStruct((tokens, hq), bf16),
            jax.ShapeDtypeStruct((tokens, hq), bf16),
            jax.ShapeDtypeStruct((PHASES, n_slots, ROWS, enc_width), bf16),
            jax.ShapeDtypeStruct((NC * n_chips, w_rows, hq // n_chips), bf16),
        ],
        in_specs=[pl.BlockSpec(memory_space=pltpu.SMEM), hbm, hbm, hbm, hbm],
        out_specs=[hbm, hbm, hbm, hbm],
        scratch_shapes=scratch,
        compiler_params=pltpu.CompilerParams(collective_id=0, has_side_effects=True, vmem_limit_bytes=62 << 20),
        name="attend_exchange",
    )(table, queries, enc_store, weight, cotangent)


def last_kernel(table_ref, back_ref, g_ref, store_ref, grad_ref, acc_ref):
    dp, fs, z, yl, core, _, _ = place()
    blk_dev = store_ref.shape[0]
    n_req = table_ref.shape[0] // (N_DP * N_FSDP)
    acc_ref[...] = jnp.zeros_like(acc_ref)

    def add(i, carry):
        dst = ((z + i // 4) % NZ) * (NY * NC) + ((yl + (i // 2) % 2) % NY) * NC + (core + i % 2) % NC
        base = (dst * N_FSDP + fs) * n_req
        a, b, count = first_two(table_ref, base, n_req, dp, Local(blk_dev))

        @pl.when(count > 0)
        def _():
            acc_ref[a] = acc_ref[a] + back_ref[0, 2 * i].astype(f32)

        @pl.when(count > 1)
        def _():
            acc_ref[b] = acc_ref[b] + back_ref[0, 2 * i + 1].astype(f32)

        return carry

    lax.fori_loop(0, N_DP, add, 0)
    store_ref[...] = acc_ref[...].astype(bf16)

    @pl.when(pl.program_id(0) == 0)
    def _():
        scale = float(n_req * N_DP * N_FSDP * BLOCK) ** (-0.5)
        cols = g_ref.shape[2]
        for half in range(NC):
            for chip in range(NZ * NY):
                grad_ref[:, half, chip * cols:(chip + 1) * cols] = g_ref[half * NZ * NY + chip].astype(f32) * scale


def last_call(table, back, grads, store_shape, w_rows, hq):
    blk_dev, _, enc_width = store_shape
    return pl.pallas_call(
        last_kernel,
        grid=(PHASES,),
        out_shape=[
            jax.ShapeDtypeStruct(store_shape, bf16),
            jax.ShapeDtypeStruct((w_rows, NC, hq), f32),
        ],
        in_specs=[
            pl.BlockSpec(memory_space=pltpu.SMEM),
            pl.BlockSpec((1,) + back.shape[1:], lambda p: (p, 0, 0, 0)),
            pl.BlockSpec(grads.shape, lambda p: (0, 0, 0)),
        ],
        out_specs=[
            pl.BlockSpec((blk_dev, ROWS, enc_width), lambda p: (0, p, 0)),
            pl.BlockSpec((w_rows, NC, hq), lambda p: (0, 0, 0)),
        ],
        scratch_shapes=[pltpu.VMEM((blk_dev, ROWS, enc_width), f32)],
        compiler_params=pltpu.CompilerParams(vmem_limit_bytes=40 << 20),
        name="store_gradient",
    )(table, back, grads)


def shards(queries, enc_store, kv_weight, table, cotangent):
    w_rows, _, hq = kv_weight.shape
    table = table.reshape(-1)
    attended, d_queries, back, grads = main_call(
        table, queries, enc_store, kv_weight.reshape(w_rows, 2 * hq), cotangent
    )
    d_store, grad_kv = last_call(table, back, grads, enc_store.shape, w_rows, hq)
    return attended, d_queries, d_store, grad_kv


def solution(mesh):
    in_specs = (
        P(("dp", "fsdp"), None),
        P(("dp", "fsdp"), None, None),
        P("fsdp", None, None),
        P(),
        P(("dp", "fsdp"), None),
    )
    out_specs = (
        P(("dp", "fsdp"), None),
        P(("dp", "fsdp"), None),
        P(("dp", "fsdp"), None, None),
        P("fsdp", None, None),
    )
    return jax.shard_map(shards, mesh=mesh, in_specs=in_specs, out_specs=out_specs, check_vma=False)
```

```python
import functools

import jax
import jax.numpy as jnp
from jax import lax
from jax.experimental import pallas as pl
from jax.experimental.pallas import tpu as pltpu
from jax.sharding import PartitionSpec as P

HEAD = 128
WIN = 64
BLOCK = 128
NEIGH = 2
CAP = 2
NZ, NY, NC = 4, 2, 2
NYH, NX = 2, 4
N_DP, N_FSDP = NZ * NY * NC, NYH * NX
PHASES = 4
ROWS = BLOCK // PHASES
SCALE = HEAD ** (-0.5)
MESH = pl.DeviceIdType.MESH
f32, bf16 = jnp.float32, jnp.bfloat16
ORDER = (
    (2, 1, 0), (2, 1, 1), (2, 0, 0), (2, 0, 1),
    (1, 1, 0), (3, 1, 0), (1, 1, 1), (3, 1, 1),
    (1, 0, 0), (3, 0, 0), (1, 0, 1), (3, 0, 1),
    (0, 1, 0), (0, 1, 1), (0, 0, 1),
)
STEPS = (2, 1, 3, 0)


def mm(a, b):
    return jnp.dot(a, b, preferred_element_type=f32)


def mm_nt(a, b):
    return lax.dot_general(a, b, (((1,), (1,)), ((), ())), preferred_element_type=f32)


def mm_tn(a, b):
    return lax.dot_general(a, b, (((0,), (0,)), ((), ())), preferred_element_type=f32)


def place():
    dp = lax.axis_index("dp")
    fs = lax.axis_index("fsdp")
    return dp, fs, dp // (NY * NC), (dp // NC) % NY, dp % NC, fs // NX, fs % NX


def two_heads(rows):
    lane = lax.broadcasted_iota(jnp.int32, rows.shape, 1)
    zero = jnp.zeros_like(rows)
    return jnp.concatenate([jnp.where(lane < HEAD, rows, zero), jnp.where(lane < HEAD, zero, rows)], axis=0)


def own_halves(full):
    return jnp.concatenate([full[:WIN, :HEAD], full[WIN:, HEAD:]], axis=1)


def pair_first(loaded):
    query, cot, keys, values = loaded
    query2, cot2 = two_heads(query), two_heads(cot)
    return query2, cot2, mm_nt(keys, query2), mm_nt(values, cot2)


def pair_softmax(first):
    query2, cot2, scores, d_probs = first
    expo = jnp.exp((scores - jnp.max(scores, axis=0, keepdims=True)) * SCALE)
    probs = expo * (1.0 / jnp.sum(expo, axis=0, keepdims=True))
    inner = jnp.sum(d_probs * probs, axis=0, keepdims=True)
    d_scores = ((probs * SCALE) * (d_probs - inner)).astype(bf16)
    return query2, cot2, probs.astype(bf16), d_scores


def pair_last(second):
    query2, cot2, probs_b, d_scores = second
    return probs_b, d_scores, mm(d_scores, query2).astype(bf16), mm(probs_b, cot2).astype(bf16)


def window_slices(win, width):
    row = pl.ds(pl.multiple_of(win * WIN, WIN), WIN)
    blk = pl.ds(win * NEIGH, NEIGH)

    def cols(pair, base):
        return pl.ds(base + pair * 2 * HEAD, 2 * HEAD)

    return row, blk, cols, width // (2 * HEAD)


def attend(win, q_ref, c_ref, kv_ref, dkv_ref, probs_ref, ds_ref):
    width = q_ref.shape[1]
    row, blk, cols, pairs = window_slices(win, width)
    keys_of = NEIGH * BLOCK
    loaded = [
        (
            q_ref[row, cols(i, 0)],
            c_ref[row, cols(i, 0)],
            kv_ref[blk, :, cols(i, 0)].reshape(keys_of, 2 * HEAD),
            kv_ref[blk, :, cols(i, width)].reshape(keys_of, 2 * HEAD),
        )
        for i in range(pairs)
    ]
    ahead = 2
    first = [pair_first(loaded[i]) for i in range(min(ahead, pairs))]
    second, last = [], []
    for i in range(pairs):
        second.append(pair_softmax(first[i]))
        if i + ahead < pairs:
            first.append(pair_first(loaded[i + ahead]))
        if i >= 1:
            last.append(pair_last(second[i - 1]))
    last.append(pair_last(second[-1]))
    for i, (probs_b, d_scores, d_key, d_value) in enumerate(last):
        probs_ref[win, i] = probs_b
        ds_ref[win, i] = d_scores
        dkv_ref[blk, :, cols(i, 0)] = d_key.reshape(NEIGH, BLOCK, 2 * HEAD)
        dkv_ref[blk, :, cols(i, width)] = d_value.reshape(NEIGH, BLOCK, 2 * HEAD)


def attend_outputs(win, kv_ref, probs_ref, ds_ref, att_ref, dq_ref):
    width = att_ref.shape[1]
    row, blk, cols, pairs = window_slices(win, width)
    keys_of = NEIGH * BLOCK
    outs = []
    for i in range(pairs):
        keys = kv_ref[blk, :, cols(i, 0)].reshape(keys_of, 2 * HEAD)
        values = kv_ref[blk, :, cols(i, width)].reshape(keys_of, 2 * HEAD)
        outs.append((own_halves(mm_tn(probs_ref[win, i], values)), own_halves(mm_tn(ds_ref[win, i], keys))))
    for i, (att, d_query) in enumerate(outs):
        att_ref[row, cols(i, 0)] = att.astype(bf16)
        dq_ref[row, cols(i, 0)] = d_query.astype(bf16)


def first_two(table_ref, device, n_req, source, blk_dev, by_request):
    first, second = jnp.int32(-1), jnp.int32(-1)
    owned = blk_dev * N_FSDP
    for r in reversed(range(n_req)):
        entry = table_ref[r % NEIGH, device * (n_req // NEIGH) + r // NEIGH]
        hit = lax.div(entry, owned) == source
        value = jnp.int32(r) if by_request else lax.rem(entry, blk_dev)
        second = jnp.where(hit, first, second)
        first = jnp.where(hit, value, first)
    return first, second


def main_kernel(
    table_ref, q_hbm, store_hbm, w_hbm, c_hbm,
    att_hbm, dq_hbm, back_hbm, grad_hbm, pick_ref,
    q_ref, c_ref, store_ref, w_raw, w_ref, send_ref, recv0, recv1, recv2, recv3,
    kv_ref, dkv_ref, probs_ref, dsc_ref, enc_ref, enc_t_ref, dn_ref,
    gs_ref, gr_ref, rs_ref, ds_ref, dr_ref, ag_ref,
    slot_ref, inv_ref,
    in_sem, out_sem, a_send, a_recv, w_send, w_recv, ws_send, ws_recv,
    b_send, b_recv, g_send, g_recv, r_send, r_recv, d_send, d_recv, o_send, o_recv, s_send, s_recv,
):
    recvs = (recv0, recv1, recv2, recv3)
    dp, fs, z, yl, core, yh, x = place()
    blk_dev = store_ref.shape[0]
    n_req = kv_ref.shape[0]
    hq = q_ref.shape[1]
    enc_width = store_ref.shape[2]
    w_rows = w_hbm.shape[0]
    w_half = w_rows // NC
    grad_cols = hq // NZ
    sib = (core + 1) % NC

    def dp_dev(dz, dy, dc):
        return (((z + dz) % NZ) * (NY * NC) + ((yl + dy) % NY) * NC + (core + dc) % NC, fs)

    def fs_dev(dyh, dx):
        ylo = (yl + dyh) % NY
        return (z * (NY * NC) + ylo * NC + core, ((yh + dyh) % NYH) * NX + (x + dx) % NX)

    FS = [(dyh, dx) for dyh in range(NYH) for dx in range(NX) if (dyh, dx) != (0, 0)]

    def remote(src, dst, ssem, rsem, dev):
        return pltpu.make_async_remote_copy(
            src_ref=src, dst_ref=dst, send_sem=ssem, recv_sem=rsem, device_id=dev, device_id_type=MESH
        )

    loads = [
        pltpu.make_async_copy(store_hbm, store_ref, in_sem.at[0]),
        pltpu.make_async_copy(w_hbm, w_raw, in_sem.at[1]),
        pltpu.make_async_copy(q_hbm, q_ref, in_sem.at[2]),
        pltpu.make_async_copy(c_hbm, c_ref, in_sem.at[3]),
    ]
    for copy in loads:
        copy.start()
    barrier = pltpu.get_barrier_semaphore()
    partners = [dp_dev(*o) for o in ORDER] + [fs_dev(*o) for o in FS]
    for dev in partners:
        pl.semaphore_signal(barrier, inc=1, device_id=dev, device_id_type=MESH)

    def picks(i, carry):
        dst = ((z + i // 4) % NZ) * (NY * NC) + ((yl + (i // 2) % 2) % NY) * NC + (core + i % 2) % NC
        a, b = first_two(table_ref, dst * N_FSDP + fs, n_req, dp, blk_dev, False)
        pick_ref[2 * i] = a
        pick_ref[2 * i + 1] = b
        return carry

    lax.fori_loop(0, N_DP, picks, 0)
    loads[0].wait()
    pl.semaphore_wait(barrier, len(partners))

    a_copies, w_copies = [], []
    for p in range(PHASES):
        rows = pl.ds(p * ROWS, ROWS)
        for dz, dy, dc in ORDER:
            i = dz * 4 + dy * 2 + dc
            for k in range(CAP):
                send_ref[p, 2 * i + k] = store_ref[jnp.maximum(pick_ref[2 * i + k], 0), rows, :]
            slot = pl.ds(2 * i, CAP)
            copy = remote(send_ref.at[p, slot], recvs[p].at[slot], a_send.at[p, i], a_recv.at[p, i], dp_dev(dz, dy, dc))
            copy.start()
            a_copies.append(copy)
        for k in range(CAP):
            recvs[p][k] = store_ref[jnp.maximum(pick_ref[k], 0), rows, :]
        if p == 0:
            loads[1].wait()
            for part in range(NC):
                for kind in range(2):
                    w_ref[fs, part, :, kind * hq:(kind + 1) * hq] = w_raw[part * w_half:(part + 1) * w_half, kind, :]
            for j, (dyh, dx) in enumerate(FS):
                part = w_ref.at[fs, core]
                copy = remote(part, part, w_send.at[j], w_recv.at[j], fs_dev(dyh, dx))
                copy.start()
                w_copies.append(copy)

    mine = dp * N_FSDP + fs

    def slots(i, carry):
        src = ((z + NZ - i // 4) % NZ) * (NY * NC) + ((yl + (i // 2) % 2) % NY) * NC + (core + i % 2) % NC
        a, b = first_two(table_ref, mine, n_req, src, blk_dev, True)
        inv_ref[2 * i] = jnp.maximum(a, 0)
        inv_ref[2 * i + 1] = jnp.maximum(b, 0)
        return carry

    lax.fori_loop(0, N_DP, slots, 0)
    sources = [
        lax.div(table_ref[r % NEIGH, mine * (n_req // NEIGH) + r // NEIGH], blk_dev * N_FSDP) for r in range(n_req)
    ]
    for r in range(n_req):
        s = sources[r]
        dz = lax.rem(z + NZ - lax.div(s, NY * NC), NZ)
        dy = lax.rem(yl + lax.rem(lax.div(s, NC), NY), NY)
        index = dz * 4 + dy * 2 + lax.rem(core + lax.rem(s, NC), NC)
        seen = jnp.int32(0)
        for earlier in range(r):
            seen = seen + (sources[earlier] == s).astype(jnp.int32)
        slot_ref[r] = index * 2 + jnp.minimum(seen, CAP - 1)

    ws_copies = []
    for j, (dyh, dx) in enumerate(FS):
        w_copies[j].wait_recv()
        src_fs = ((yh + dyh) % NYH) * NX + (x + NX - dx) % NX
        part = w_ref.at[src_fs, core]
        copy = remote(part, part, ws_send.at[j], ws_recv.at[j], dp_dev(0, 0, 1))
        copy.start()
        ws_copies.append(copy)
    for copy in ws_copies:
        copy.wait_recv()

    for p in range(PHASES):
        for copy in a_copies[p * len(ORDER):(p + 1) * len(ORDER)]:
            copy.wait_recv()
        rows = pl.ds(p * ROWS, ROWS)
        for r in range(n_req):
            enc_ref[p, r] = recvs[p][slot_ref[r]]

        @pl.loop(0, kv_ref.shape[2] // 1024)
        def _(t):
            c = pl.ds(pl.multiple_of(t * 1024, 1024), 1024)
            out = mm(enc_ref[p].reshape(n_req * ROWS, enc_width), w_ref[:, :, :, c].reshape(enc_width, 1024))
            kv_ref[:, rows, c] = out.astype(bf16).reshape(n_req, ROWS, 1024)

    loads[2].wait()
    loads[3].wait()

    @pl.loop(0, n_req // NEIGH)
    def _(win):
        attend(win, q_ref, c_ref, kv_ref, dkv_ref, probs_ref, dsc_ref)

    outs = []
    for copy in a_copies:
        copy.wait_send()

    b_copies = []

    def d_neigh(p):
        rows = pl.ds(p * ROWS, ROWS)
        lhs = dkv_ref[:, rows, :].reshape(n_req * ROWS, 2 * hq)

        @pl.loop(0, 2)
        def _(t):
            part = w_ref[pl.ds(t * (N_FSDP // 2), N_FSDP // 2)].reshape(enc_width // 2, 2 * hq)
            c = pl.ds(pl.multiple_of(t * (enc_width // 2), enc_width // 2), enc_width // 2)
            dn_ref[:, :, c] = mm_nt(lhs, part).astype(bf16).reshape(n_req, ROWS, enc_width // 2)

        for i in range(N_DP):
            for k in range(CAP):
                send_ref[p, 2 * i + k] = dn_ref[inv_ref[2 * i + k]]
        slot = pl.ds(0, CAP)
        copy = pltpu.make_async_copy(send_ref.at[p, slot], back_hbm.at[p, slot], out_sem.at[2 + p])
        copy.start()
        outs.append(copy)

    pending = [(p, offset) for p in range(PHASES) for offset in ORDER]

    def send_back(count):
        for _ in range(count):
            p, (dz, dy, dc) = pending[len(b_copies)]
            i = dz * 4 + dy * 2 + dc
            slot = pl.ds(2 * i, CAP)
            copy = remote(
                send_ref.at[p, slot], back_hbm.at[p, slot], b_send.at[p, i], b_recv.at[p, i],
                dp_dev((NZ - dz) % NZ, dy, dc),
            )
            copy.start()
            b_copies.append(copy)

    b_sent = []

    def wait_sent(count):
        for _ in range(count):
            b_copies[len(b_sent)].wait_send()
            b_sent.append(1)

    def grad_tile(half, t):
        tile = (z + STEPS[t]) % NZ
        c = pl.ds(pl.multiple_of(half * hq + tile * grad_cols, grad_cols), grad_cols)
        return mm(enc_t_ref[...], dkv_ref[:, :, c].reshape(n_req * BLOCK, grad_cols)).reshape(
            N_FSDP, w_rows, grad_cols
        )

    g_copies, r_copies = [], []

    def for_sibling(t):
        gs_ref[t] = grad_tile(sib, t).astype(bf16)
        copy = remote(gs_ref.at[t], gr_ref.at[t], g_send.at[t], g_recv.at[t], dp_dev(0, 0, 1))
        copy.start()
        g_copies.append(copy)

    def for_owners(t):
        own = grad_tile(core, t)
        g_copies[t].wait()
        gs_ref[t] = (own + gr_ref[t].astype(f32)).astype(bf16)
        for j, (dyh, dx) in enumerate(FS):
            dst_fs = ((yh + dyh) % NYH) * NX + (x + dx) % NX
            copy = remote(gs_ref.at[t, dst_fs], rs_ref.at[t, j], r_send.at[t, j], r_recv.at[t, j], fs_dev(dyh, dx))
            copy.start()
            r_copies.append(copy)

    part_cols = grad_cols // NY
    d_copies = []

    def reduce_tile(t):
        for copy in r_copies[t * len(FS):(t + 1) * len(FS)]:
            copy.wait_recv()
        total = gs_ref[t, fs].astype(f32)
        for j in range(len(FS)):
            total = total + rs_ref[t, j].astype(f32)
        for s in range(NY):
            ds_ref[t, s] = total[:, s * part_cols:(s + 1) * part_cols].astype(bf16)
        for dy in range(NY):
            m = len(d_copies)
            if (STEPS[t], dy) != (0, 0):
                copy = remote(
                    ds_ref.at[t, (yl + dy) % NY], dr_ref.at[m], d_send.at[m], d_recv.at[m], dp_dev(STEPS[t], dy, 0)
                )
                copy.start()
                d_copies.append(copy)

    d_neigh(0)
    send_back(15)
    enc_rows = jnp.concatenate([enc_ref[p] for p in range(PHASES)], axis=1).reshape(n_req * BLOCK, enc_width)
    enc_t_ref[...] = enc_rows.T
    for_sibling(0)
    for_sibling(1)
    for_owners(0)
    for_owners(1)
    d_neigh(1)
    send_back(15)
    for_sibling(2)
    for_sibling(3)
    for_owners(2)
    for_owners(3)
    d_neigh(2)
    d_neigh(3)

    @pl.loop(0, n_req // NEIGH)
    def _(win):
        attend_outputs(win, kv_ref, probs_ref, dsc_ref, q_ref, c_ref)

    for k, (src, dst) in enumerate(((q_ref, att_hbm), (c_ref, dq_hbm))):
        copy = pltpu.make_async_copy(src, dst, out_sem.at[k])
        copy.start()
        outs.append(copy)
    reduce_tile(0)
    wait_sent(15)
    send_back(8)
    reduce_tile(1)
    reduce_tile(2)
    wait_sent(8)
    send_back(7)
    reduce_tile(3)
    send_back(8)

    own_chip = z * NY + yl
    chips = [(dz, dy) for dz in range(NZ) for dy in range(NY) if (dz, dy) != (0, 0)]
    total = ds_ref[STEPS.index(0), yl].astype(f32)
    for m in range(len(chips)):
        d_copies[m].wait_recv()
        total = total + dr_ref[m].astype(f32)
    ag_ref[...] = total.astype(bf16)

    def piece(chip):
        return grad_hbm.at[core * (NZ * NY) + chip]

    copy = pltpu.make_async_copy(ag_ref, piece(own_chip), out_sem.at[2 + PHASES])
    copy.start()
    outs.append(copy)
    o_copies, s_copies = [], []
    for m, (dz, dy) in enumerate(chips):
        copy = remote(ag_ref, piece(own_chip), o_send.at[m], o_recv.at[m], dp_dev(dz, dy, 0))
        copy.start()
        o_copies.append(copy)
    copy = remote(ag_ref, piece(own_chip), s_send.at[len(chips)], s_recv.at[len(chips)], dp_dev(0, 0, 1))
    copy.start()
    s_copies.append(copy)
    send_back(len(pending) - len(b_copies))
    for m, (dz, dy) in enumerate(chips):
        o_copies[m].wait_recv()
        part = piece(((z + NZ - dz) % NZ) * NY + (yl + dy) % NY)
        copy = remote(part, part, s_send.at[m], s_recv.at[m], dp_dev(0, 0, 1))
        copy.start()
        s_copies.append(copy)
    for copy in outs:
        copy.wait()
    for copy in w_copies + ws_copies + r_copies + d_copies + o_copies + b_copies[len(b_sent):]:
        copy.wait_send()
    for copy in b_copies:
        copy.wait_recv()
    for copy in s_copies:
        copy.wait()


def main_call(table, queries, enc_store, weight, cotangent):
    tokens, hq = queries.shape
    blk_dev, _, enc_width = enc_store.shape
    n_req = tokens // WIN * NEIGH
    w_rows = weight.shape[0]
    n_slots = N_DP * CAP
    n_tiles, grad_cols, pairs = NZ, hq // NZ, hq // (2 * HEAD)
    n_chips = NZ * NY
    hbm = pl.BlockSpec(memory_space=pl.ANY)
    vm = pltpu.VMEM
    sem = pltpu.SemaphoreType.DMA
    recv = vm((n_slots, ROWS, enc_width), bf16)
    scratch = [
        vm((tokens, hq), bf16), vm((tokens, hq), bf16), vm(enc_store.shape, bf16),
        vm(weight.shape, bf16), vm((N_FSDP, NC, w_rows // NC, 2 * hq), bf16), vm((PHASES, n_slots, ROWS, enc_width), bf16),
        recv, recv, recv, recv,
        vm((n_req, BLOCK, 2 * hq), bf16), vm((n_req, BLOCK, 2 * hq), bf16),
        vm((n_req // NEIGH, pairs, NEIGH * BLOCK, 2 * WIN), bf16),
        vm((n_req // NEIGH, pairs, NEIGH * BLOCK, 2 * WIN), bf16), vm((PHASES, n_req, ROWS, enc_width), bf16),
        vm((enc_width, n_req * BLOCK), bf16),
        vm((n_req, ROWS, enc_width), bf16),
        vm((n_tiles, N_FSDP, w_rows, grad_cols), bf16),
        vm((n_tiles, N_FSDP, w_rows, grad_cols), bf16), vm((n_tiles, N_FSDP - 1, w_rows, grad_cols), bf16),
        vm((NZ, NY, w_rows, hq // n_chips), bf16), vm((n_chips - 1, w_rows, hq // n_chips), bf16),
        vm((w_rows, hq // n_chips), bf16),
        pltpu.SMEM((n_req,), jnp.int32), pltpu.SMEM((n_slots,), jnp.int32),
        sem((4,)), sem((3 + PHASES,)), sem((PHASES, N_DP)), sem((PHASES, N_DP)),
        sem((N_FSDP - 1,)), sem((N_FSDP - 1,)), sem((N_FSDP - 1,)), sem((N_FSDP - 1,)),
        sem((PHASES, N_DP)), sem((PHASES, N_DP)), sem((n_tiles,)), sem((n_tiles,)),
        sem((n_tiles, N_FSDP - 1)), sem((n_tiles, N_FSDP - 1)), sem((n_chips - 1,)), sem((n_chips - 1,)),
        sem((n_chips - 1,)), sem((n_chips - 1,)), sem((n_chips,)), sem((n_chips,)),
    ]
    return pl.pallas_call(
        main_kernel,
        out_shape=[
            jax.ShapeDtypeStruct((tokens, hq), bf16),
            jax.ShapeDtypeStruct((tokens, hq), bf16),
            jax.ShapeDtypeStruct((PHASES, n_slots, ROWS, enc_width), bf16),
            jax.ShapeDtypeStruct((NC * n_chips, w_rows, hq // n_chips), bf16),
            jax.ShapeDtypeStruct((n_slots,), jnp.int32),
        ],
        in_specs=[pl.BlockSpec(memory_space=pltpu.SMEM), hbm, hbm, hbm, hbm],
        out_specs=[hbm, hbm, hbm, hbm, pl.BlockSpec(memory_space=pltpu.SMEM)],
        scratch_shapes=scratch,
        compiler_params=pltpu.CompilerParams(collective_id=0, has_side_effects=True, vmem_limit_bytes=63 << 20),
        name="attend_exchange",
    )(table, queries, enc_store, weight, cotangent)


def last_kernel(
    scale, pick_ref, back_ref, g_ref, att_in, dq_in, store_ref, grad_ref, att_out, dq_out, acc_ref
):
    att_out[...] = att_in[...]
    dq_out[...] = dq_in[...]
    acc_ref[...] = jnp.zeros_like(acc_ref)
    for i in range(pick_ref.shape[0]):
        @pl.when(pick_ref[i] >= 0)
        def _():
            acc_ref[pick_ref[i]] += back_ref[0, i].astype(f32)

    store_ref[...] = acc_ref[...].astype(bf16)

    @pl.when(pl.program_id(0) == 0)
    def _():
        cols = g_ref.shape[2]
        for half in range(NC):
            for chip in range(NZ * NY):
                grad_ref[:, half, chip * cols:(chip + 1) * cols] = g_ref[half * NZ * NY + chip].astype(f32) * scale


def last_call(picks, back, grads, attended, d_queries, store_shape, w_rows, hq):
    blk_dev, _, enc_width = store_shape
    tokens = attended.shape[0]
    rows = pl.BlockSpec((tokens // PHASES, hq), lambda p: (p, 0))
    scale = float(tokens // WIN * NEIGH * BLOCK * N_DP * N_FSDP) ** (-0.5)
    return pl.pallas_call(
        functools.partial(last_kernel, scale),
        grid=(PHASES,),
        out_shape=[
            jax.ShapeDtypeStruct(store_shape, bf16),
            jax.ShapeDtypeStruct((w_rows, NC, hq), f32),
            jax.ShapeDtypeStruct(attended.shape, bf16),
            jax.ShapeDtypeStruct(d_queries.shape, bf16),
        ],
        in_specs=[
            pl.BlockSpec(memory_space=pltpu.SMEM),
            pl.BlockSpec((1,) + back.shape[1:], lambda p: (p, 0, 0, 0)),
            pl.BlockSpec(grads.shape, lambda p: (0, 0, 0)),
            rows, rows,
        ],
        out_specs=[
            pl.BlockSpec((blk_dev, ROWS, enc_width), lambda p: (0, p, 0)),
            pl.BlockSpec((w_rows, NC, hq), lambda p: (0, 0, 0)),
            rows, rows,
        ],
        scratch_shapes=[pltpu.VMEM((blk_dev, ROWS, enc_width), f32)],
        compiler_params=pltpu.CompilerParams(vmem_limit_bytes=62 << 20),
        name="store_gradient",
    )(picks, back, grads, attended, d_queries)


def shards(queries, enc_store, kv_weight, table, cotangent):
    w_rows, _, hq = kv_weight.shape
    attended, d_queries, back, grads, picks = main_call(table.T, queries, enc_store, kv_weight, cotangent)
    d_store, grad_kv, attended, d_queries = last_call(
        picks, back, grads, attended, d_queries, enc_store.shape, w_rows, hq
    )
    return attended, d_queries, d_store, grad_kv


def solution(mesh):
    in_specs = (
        P(("dp", "fsdp"), None),
        P(("dp", "fsdp"), None, None),
        P("fsdp", None, None),
        P(),
        P(("dp", "fsdp"), None),
    )
    out_specs = (
        P(("dp", "fsdp"), None),
        P(("dp", "fsdp"), None),
        P(("dp", "fsdp"), None, None),
        P("fsdp", None, None),
    )
    return jax.shard_map(shards, mesh=mesh, in_specs=in_specs, out_specs=out_specs, check_vma=False)
```

```python
import functools

import jax
import jax.numpy as jnp
from jax import lax
from jax.experimental import pallas as pl
from jax.experimental.pallas import tpu as pltpu
from jax.sharding import PartitionSpec as P

HEAD = 128
WIN = 64
BLOCK = 128
NEIGH = 2
CAP = 2
NZ, NY, NC = 4, 2, 2
NYH, NX = 2, 4
N_DP, N_FSDP = NZ * NY * NC, NYH * NX
PHASES = 4
ROWS = BLOCK // PHASES
SCALE = HEAD ** (-0.5)
LOG2E = 1.4426950408889634
MESH = pl.DeviceIdType.MESH
f32, bf16 = jnp.float32, jnp.bfloat16
ORDER = (
    (2, 1, 0), (2, 1, 1), (2, 0, 0), (2, 0, 1),
    (1, 1, 0), (3, 1, 0), (1, 1, 1), (3, 1, 1),
    (1, 0, 0), (3, 0, 0), (1, 0, 1), (3, 0, 1),
    (0, 1, 0), (0, 1, 1), (0, 0, 1),
)
STEPS = (2, 1, 3, 0)


def mm(a, b):
    return jnp.dot(a, b, preferred_element_type=f32)


def mm_nt(a, b):
    return lax.dot_general(a, b, (((1,), (1,)), ((), ())), preferred_element_type=f32)


def mm_tn(a, b):
    return lax.dot_general(a, b, (((0,), (0,)), ((), ())), preferred_element_type=f32)


def place():
    dp = lax.axis_index("dp")
    fs = lax.axis_index("fsdp")
    return dp, fs, dp // (NY * NC), (dp // NC) % NY, dp % NC, fs // NX, fs % NX


def two_heads(rows):
    lane = lax.broadcasted_iota(jnp.int32, rows.shape, 1)
    zero = jnp.zeros_like(rows)
    return jnp.concatenate([jnp.where(lane < HEAD, rows, zero), jnp.where(lane < HEAD, zero, rows)], axis=0)


def own_halves(full):
    return jnp.concatenate([full[:WIN, :HEAD], full[WIN:, HEAD:]], axis=1)


def pair_first(loaded):
    query, cot, keys, values = loaded
    query2, cot2 = two_heads(query), two_heads(cot)
    return query2, cot2, mm_nt(keys, query2), mm_nt(values, cot2)


def pair_softmax(first):
    query2, cot2, scores, d_probs = first
    expo = jnp.exp2((scores - jnp.max(scores, axis=0, keepdims=True)) * (SCALE * LOG2E))
    probs = expo * (1.0 / jnp.sum(expo, axis=0, keepdims=True))
    inner = jnp.sum(d_probs * probs, axis=0, keepdims=True)
    d_scores = ((probs * SCALE) * (d_probs - inner)).astype(bf16)
    return query2, cot2, probs.astype(bf16), d_scores


def pair_last(second):
    query2, cot2, probs_b, d_scores = second
    return probs_b, d_scores, mm(d_scores, query2).astype(bf16), mm(probs_b, cot2).astype(bf16)


def window_slices(win, width):
    row = pl.ds(pl.multiple_of(win * WIN, WIN), WIN)
    blk = pl.ds(win * NEIGH, NEIGH)

    def cols(pair, base):
        return pl.ds(base + pair * 2 * HEAD, 2 * HEAD)

    return row, blk, cols, width // (2 * HEAD)


def attend(wins, q_ref, c_ref, kv_ref, dkv_ref, probs_ref, ds_ref):
    width = q_ref.shape[1]
    keys_of = NEIGH * BLOCK
    items, loaded = [], []
    for win in wins:
        row, blk, cols, pairs = window_slices(win, width)
        for i in range(pairs):
            items.append((win, blk, i, cols(i, 0), cols(i, width)))
            loaded.append(
                (
                    q_ref[row, cols(i, 0)],
                    c_ref[row, cols(i, 0)],
                    kv_ref[blk, :, cols(i, 0)].reshape(keys_of, 2 * HEAD),
                    kv_ref[blk, :, cols(i, width)].reshape(keys_of, 2 * HEAD),
                )
            )
    count = len(items)
    ahead = 2
    first = [pair_first(loaded[i]) for i in range(ahead)]
    second, last = [], []
    for i in range(count):
        second.append(pair_softmax(first[i]))
        if i + ahead < count:
            first.append(pair_first(loaded[i + ahead]))
        if i >= 1:
            last.append(pair_last(second[i - 1]))
    last.append(pair_last(second[-1]))
    for (win, blk, i, key_cols, value_cols), (probs_b, d_scores, d_key, d_value) in zip(items, last):
        probs_ref[win, i] = probs_b
        ds_ref[win, i] = d_scores
        dkv_ref[blk, :, key_cols] = d_key.reshape(NEIGH, BLOCK, 2 * HEAD)
        dkv_ref[blk, :, value_cols] = d_value.reshape(NEIGH, BLOCK, 2 * HEAD)


def attend_outputs(win, kv_ref, probs_ref, ds_ref, att_ref, dq_ref):
    width = att_ref.shape[1]
    row, blk, cols, pairs = window_slices(win, width)
    keys_of = NEIGH * BLOCK
    outs = []
    for i in range(pairs):
        keys = kv_ref[blk, :, cols(i, 0)].reshape(keys_of, 2 * HEAD)
        values = kv_ref[blk, :, cols(i, width)].reshape(keys_of, 2 * HEAD)
        outs.append((own_halves(mm_tn(probs_ref[win, i], values)), own_halves(mm_tn(ds_ref[win, i], keys))))
    for i, (att, d_query) in enumerate(outs):
        att_ref[row, cols(i, 0)] = att.astype(bf16)
        dq_ref[row, cols(i, 0)] = d_query.astype(bf16)


def first_two(table_ref, device, n_req, source, blk_dev, by_request):
    first, second = jnp.int32(-1), jnp.int32(-1)
    owned = blk_dev * N_FSDP
    for r in reversed(range(n_req)):
        entry = table_ref[r % NEIGH, device * (n_req // NEIGH) + r // NEIGH]
        hit = lax.div(entry, owned) == source
        value = jnp.int32(r) if by_request else lax.rem(entry, blk_dev)
        second = jnp.where(hit, first, second)
        first = jnp.where(hit, value, first)
    return first, second


def main_kernel(
    table_ref, q_hbm, store_hbm, w_hbm, c_hbm,
    att_hbm, dq_hbm, back_hbm, grad_hbm, pick_ref,
    q_ref, c_ref, store_ref, w_raw, w_ref, send_ref, recv0, recv1, recv2, recv3,
    kv_ref, dkv_ref, probs_ref, dsc_ref, enc_ref, enc_t_ref, dn_ref,
    gs_ref, gr_ref, rs_ref, ds_ref, dr_ref, ag_ref,
    slot_ref, inv_ref,
    in_sem, out_sem, a_send, a_recv, w_send, w_recv, ws_send, ws_recv,
    b_send, b_recv, g_send, g_recv, r_send, r_recv, d_send, d_recv, o_send, o_recv, s_send, s_recv,
):
    recvs = (recv0, recv1, recv2, recv3)
    dp, fs, z, yl, core, yh, x = place()
    blk_dev = store_ref.shape[0]
    n_req = kv_ref.shape[0]
    hq = q_ref.shape[1]
    enc_width = store_ref.shape[2]
    w_rows = w_hbm.shape[0]
    w_half = w_rows // NC
    grad_cols = hq // NZ
    sib = (core + 1) % NC

    def dp_dev(dz, dy, dc):
        return (((z + dz) % NZ) * (NY * NC) + ((yl + dy) % NY) * NC + (core + dc) % NC, fs)

    def fs_dev(dyh, dx):
        ylo = (yl + dyh) % NY
        return (z * (NY * NC) + ylo * NC + core, ((yh + dyh) % NYH) * NX + (x + dx) % NX)

    FS = [(dyh, dx) for dyh in range(NYH) for dx in range(NX) if (dyh, dx) != (0, 0)]

    def remote(src, dst, ssem, rsem, dev):
        return pltpu.make_async_remote_copy(
            src_ref=src, dst_ref=dst, send_sem=ssem, recv_sem=rsem, device_id=dev, device_id_type=MESH
        )

    loads = [
        pltpu.make_async_copy(store_hbm, store_ref, in_sem.at[0]),
        pltpu.make_async_copy(w_hbm, w_raw, in_sem.at[1]),
        pltpu.make_async_copy(q_hbm, q_ref, in_sem.at[2]),
        pltpu.make_async_copy(c_hbm, c_ref, in_sem.at[3]),
    ]
    for copy in loads:
        copy.start()
    barrier = pltpu.get_barrier_semaphore()
    partners = [dp_dev(*o) for o in ORDER] + [fs_dev(*o) for o in FS]
    for dev in partners:
        pl.semaphore_signal(barrier, inc=1, device_id=dev, device_id_type=MESH)

    def picks(i, carry):
        dst = ((z + i // 4) % NZ) * (NY * NC) + ((yl + (i // 2) % 2) % NY) * NC + (core + i % 2) % NC
        a, b = first_two(table_ref, dst * N_FSDP + fs, n_req, dp, blk_dev, False)
        pick_ref[2 * i] = a
        pick_ref[2 * i + 1] = b
        return carry

    lax.fori_loop(0, N_DP, picks, 0)
    loads[0].wait()
    pl.semaphore_wait(barrier, len(partners))

    a_copies, w_copies = [], []
    for p in range(PHASES):
        rows = pl.ds(p * ROWS, ROWS)
        for dz, dy, dc in ORDER:
            i = dz * 4 + dy * 2 + dc
            for k in range(CAP):
                send_ref[p, 2 * i + k] = store_ref[jnp.maximum(pick_ref[2 * i + k], 0), rows, :]
            slot = pl.ds(2 * i, CAP)
            copy = remote(send_ref.at[p, slot], recvs[p].at[slot], a_send.at[p, i], a_recv.at[p, i], dp_dev(dz, dy, dc))
            copy.start()
            a_copies.append(copy)
        for k in range(CAP):
            recvs[p][k] = store_ref[jnp.maximum(pick_ref[k], 0), rows, :]
        if p == 0:
            loads[1].wait()
            for part in range(NC):
                for kind in range(2):
                    w_ref[fs, part, :, kind * hq:(kind + 1) * hq] = w_raw[part * w_half:(part + 1) * w_half, kind, :]
            for j, (dyh, dx) in enumerate(FS):
                part = w_ref.at[fs, core]
                copy = remote(part, part, w_send.at[j], w_recv.at[j], fs_dev(dyh, dx))
                copy.start()
                w_copies.append(copy)

    mine = dp * N_FSDP + fs

    def slots(i, carry):
        src = ((z + NZ - i // 4) % NZ) * (NY * NC) + ((yl + (i // 2) % 2) % NY) * NC + (core + i % 2) % NC
        a, b = first_two(table_ref, mine, n_req, src, blk_dev, True)
        inv_ref[2 * i] = jnp.maximum(a, 0)
        inv_ref[2 * i + 1] = jnp.maximum(b, 0)
        return carry

    lax.fori_loop(0, N_DP, slots, 0)
    sources = [
        lax.div(table_ref[r % NEIGH, mine * (n_req // NEIGH) + r // NEIGH], blk_dev * N_FSDP) for r in range(n_req)
    ]
    for r in range(n_req):
        s = sources[r]
        dz = lax.rem(z + NZ - lax.div(s, NY * NC), NZ)
        dy = lax.rem(yl + lax.rem(lax.div(s, NC), NY), NY)
        index = dz * 4 + dy * 2 + lax.rem(core + lax.rem(s, NC), NC)
        seen = jnp.int32(0)
        for earlier in range(r):
            seen = seen + (sources[earlier] == s).astype(jnp.int32)
        slot_ref[r] = index * 2 + jnp.minimum(seen, CAP - 1)

    ws_copies = []
    for j, (dyh, dx) in enumerate(FS):
        w_copies[j].wait_recv()
        src_fs = ((yh + dyh) % NYH) * NX + (x + NX - dx) % NX
        part = w_ref.at[src_fs, core]
        copy = remote(part, part, ws_send.at[j], ws_recv.at[j], dp_dev(0, 0, 1))
        copy.start()
        ws_copies.append(copy)
    for copy in ws_copies:
        copy.wait_recv()

    for p in range(PHASES):
        for copy in a_copies[p * len(ORDER):(p + 1) * len(ORDER)]:
            copy.wait_recv()
        rows = pl.ds(p * ROWS, ROWS)
        for r in range(n_req):
            enc_ref[p, r] = recvs[p][slot_ref[r]]

        @pl.loop(0, kv_ref.shape[2] // 1024)
        def _(t):
            c = pl.ds(pl.multiple_of(t * 1024, 1024), 1024)
            out = mm(enc_ref[p].reshape(n_req * ROWS, enc_width), w_ref[:, :, :, c].reshape(enc_width, 1024))
            kv_ref[:, rows, c] = out.astype(bf16).reshape(n_req, ROWS, 1024)

    loads[2].wait()
    loads[3].wait()

    together = 3

    @pl.loop(0, n_req // NEIGH // together)
    def _(step):
        attend([step * together + k for k in range(together)], q_ref, c_ref, kv_ref, dkv_ref, probs_ref, dsc_ref)

    outs = []
    for copy in a_copies:
        copy.wait_send()

    b_copies = []

    def d_neigh(p):
        rows = pl.ds(p * ROWS, ROWS)
        lhs = dkv_ref[:, rows, :].reshape(n_req * ROWS, 2 * hq)

        @pl.loop(0, 2)
        def _(t):
            part = w_ref[pl.ds(t * (N_FSDP // 2), N_FSDP // 2)].reshape(enc_width // 2, 2 * hq)
            c = pl.ds(pl.multiple_of(t * (enc_width // 2), enc_width // 2), enc_width // 2)
            dn_ref[:, :, c] = mm_nt(lhs, part).astype(bf16).reshape(n_req, ROWS, enc_width // 2)

        for i in range(N_DP):
            for k in range(CAP):
                send_ref[p, 2 * i + k] = dn_ref[inv_ref[2 * i + k]]
        slot = pl.ds(0, CAP)
        copy = pltpu.make_async_copy(send_ref.at[p, slot], back_hbm.at[p, slot], out_sem.at[2 + p])
        copy.start()
        outs.append(copy)

    pending = [(p, offset) for p in range(PHASES) for offset in ORDER]

    def send_back(count):
        for _ in range(count):
            p, (dz, dy, dc) = pending[len(b_copies)]
            i = dz * 4 + dy * 2 + dc
            slot = pl.ds(2 * i, CAP)
            copy = remote(
                send_ref.at[p, slot], back_hbm.at[p, slot], b_send.at[p, i], b_recv.at[p, i],
                dp_dev((NZ - dz) % NZ, dy, dc),
            )
            copy.start()
            b_copies.append(copy)

    b_sent = []

    def wait_sent(count):
        for _ in range(count):
            b_copies[len(b_sent)].wait_send()
            b_sent.append(1)

    def grad_tile(half, t):
        tile = (z + STEPS[t]) % NZ
        c = pl.ds(pl.multiple_of(half * hq + tile * grad_cols, grad_cols), grad_cols)
        return mm(enc_t_ref[...], dkv_ref[:, :, c].reshape(n_req * BLOCK, grad_cols)).reshape(
            N_FSDP, w_rows, grad_cols
        )

    g_copies, r_copies = [], []

    def for_sibling(t):
        gs_ref[t] = grad_tile(sib, t).astype(bf16)
        copy = remote(gs_ref.at[t], gr_ref.at[t], g_send.at[t], g_recv.at[t], dp_dev(0, 0, 1))
        copy.start()
        g_copies.append(copy)

    def for_owners(t):
        own = grad_tile(core, t)
        g_copies[t].wait()
        gs_ref[t] = (own + gr_ref[t].astype(f32)).astype(bf16)
        for j, (dyh, dx) in enumerate(FS):
            dst_fs = ((yh + dyh) % NYH) * NX + (x + dx) % NX
            copy = remote(gs_ref.at[t, dst_fs], rs_ref.at[t, j], r_send.at[t, j], r_recv.at[t, j], fs_dev(dyh, dx))
            copy.start()
            r_copies.append(copy)

    part_cols = grad_cols // NY
    d_copies = []

    def reduce_tile(t):
        for copy in r_copies[t * len(FS):(t + 1) * len(FS)]:
            copy.wait_recv()
        total = gs_ref[t, fs].astype(f32)
        for j in range(len(FS)):
            total = total + rs_ref[t, j].astype(f32)
        for s in range(NY):
            ds_ref[t, s] = total[:, s * part_cols:(s + 1) * part_cols].astype(bf16)
        for dy in range(NY):
            m = len(d_copies)
            if (STEPS[t], dy) != (0, 0):
                copy = remote(
                    ds_ref.at[t, (yl + dy) % NY], dr_ref.at[m], d_send.at[m], d_recv.at[m], dp_dev(STEPS[t], dy, 0)
                )
                copy.start()
                d_copies.append(copy)

    d_neigh(0)
    send_back(15)
    enc_rows = jnp.concatenate([enc_ref[p] for p in range(PHASES)], axis=1).reshape(n_req * BLOCK, enc_width)
    enc_t_ref[...] = enc_rows.T
    for_sibling(0)
    for_sibling(1)
    for_owners(0)
    for_owners(1)
    d_neigh(1)
    send_back(15)
    for_sibling(2)
    for_sibling(3)
    for_owners(2)
    for_owners(3)
    d_neigh(2)
    d_neigh(3)

    @pl.loop(0, n_req // NEIGH)
    def _(win):
        attend_outputs(win, kv_ref, probs_ref, dsc_ref, q_ref, c_ref)

    for k, (src, dst) in enumerate(((q_ref, att_hbm), (c_ref, dq_hbm))):
        copy = pltpu.make_async_copy(src, dst, out_sem.at[k])
        copy.start()
        outs.append(copy)
    reduce_tile(0)
    wait_sent(15)
    send_back(8)
    reduce_tile(1)
    reduce_tile(2)
    wait_sent(8)
    send_back(7)
    reduce_tile(3)
    send_back(8)

    own_chip = z * NY + yl
    chips = [(dz, dy) for dz in range(NZ) for dy in range(NY) if (dz, dy) != (0, 0)]
    total = ds_ref[STEPS.index(0), yl].astype(f32)
    for m in range(len(chips)):
        d_copies[m].wait_recv()
        total = total + dr_ref[m].astype(f32)
    ag_ref[...] = total.astype(bf16)

    def piece(chip):
        return grad_hbm.at[core * (NZ * NY) + chip]

    copy = pltpu.make_async_copy(ag_ref, piece(own_chip), out_sem.at[2 + PHASES])
    copy.start()
    outs.append(copy)
    o_copies, s_copies = [], []
    for m, (dz, dy) in enumerate(chips):
        copy = remote(ag_ref, piece(own_chip), o_send.at[m], o_recv.at[m], dp_dev(dz, dy, 0))
        copy.start()
        o_copies.append(copy)
    copy = remote(ag_ref, piece(own_chip), s_send.at[len(chips)], s_recv.at[len(chips)], dp_dev(0, 0, 1))
    copy.start()
    s_copies.append(copy)
    send_back(len(pending) - len(b_copies))
    for m, (dz, dy) in enumerate(chips):
        o_copies[m].wait_recv()
        part = piece(((z + NZ - dz) % NZ) * NY + (yl + dy) % NY)
        copy = remote(part, part, s_send.at[m], s_recv.at[m], dp_dev(0, 0, 1))
        copy.start()
        s_copies.append(copy)
    for copy in outs:
        copy.wait()
    for copy in w_copies + ws_copies + r_copies + d_copies + o_copies + b_copies[len(b_sent):]:
        copy.wait_send()
    for copy in b_copies:
        copy.wait_recv()
    for copy in s_copies:
        copy.wait()


def main_call(table, queries, enc_store, weight, cotangent):
    tokens, hq = queries.shape
    blk_dev, _, enc_width = enc_store.shape
    n_req = tokens // WIN * NEIGH
    w_rows = weight.shape[0]
    n_slots = N_DP * CAP
    n_tiles, grad_cols, pairs = NZ, hq // NZ, hq // (2 * HEAD)
    n_chips = NZ * NY
    hbm = pl.BlockSpec(memory_space=pl.ANY)
    vm = pltpu.VMEM
    sem = pltpu.SemaphoreType.DMA
    recv = vm((n_slots, ROWS, enc_width), bf16)
    scratch = [
        vm((tokens, hq), bf16), vm((tokens, hq), bf16), vm(enc_store.shape, bf16),
        vm(weight.shape, bf16), vm((N_FSDP, NC, w_rows // NC, 2 * hq), bf16), vm((PHASES, n_slots, ROWS, enc_width), bf16),
        recv, recv, recv, recv,
        vm((n_req, BLOCK, 2 * hq), bf16), vm((n_req, BLOCK, 2 * hq), bf16),
        vm((n_req // NEIGH, pairs, NEIGH * BLOCK, 2 * WIN), bf16),
        vm((n_req // NEIGH, pairs, NEIGH * BLOCK, 2 * WIN), bf16), vm((PHASES, n_req, ROWS, enc_width), bf16),
        vm((enc_width, n_req * BLOCK), bf16),
        vm((n_req, ROWS, enc_width), bf16),
        vm((n_tiles, N_FSDP, w_rows, grad_cols), bf16),
        vm((n_tiles, N_FSDP, w_rows, grad_cols), bf16), vm((n_tiles, N_FSDP - 1, w_rows, grad_cols), bf16),
        vm((NZ, NY, w_rows, hq // n_chips), bf16), vm((n_chips - 1, w_rows, hq // n_chips), bf16),
        vm((w_rows, hq // n_chips), bf16),
        pltpu.SMEM((n_req,), jnp.int32), pltpu.SMEM((n_slots,), jnp.int32),
        sem((4,)), sem((3 + PHASES,)), sem((PHASES, N_DP)), sem((PHASES, N_DP)),
        sem((N_FSDP - 1,)), sem((N_FSDP - 1,)), sem((N_FSDP - 1,)), sem((N_FSDP - 1,)),
        sem((PHASES, N_DP)), sem((PHASES, N_DP)), sem((n_tiles,)), sem((n_tiles,)),
        sem((n_tiles, N_FSDP - 1)), sem((n_tiles, N_FSDP - 1)), sem((n_chips - 1,)), sem((n_chips - 1,)),
        sem((n_chips - 1,)), sem((n_chips - 1,)), sem((n_chips,)), sem((n_chips,)),
    ]
    return pl.pallas_call(
        main_kernel,
        out_shape=[
            jax.ShapeDtypeStruct((tokens, hq), bf16),
            jax.ShapeDtypeStruct((tokens, hq), bf16),
            jax.ShapeDtypeStruct((PHASES, n_slots, ROWS, enc_width), bf16),
            jax.ShapeDtypeStruct((NC * n_chips, w_rows, hq // n_chips), bf16),
            jax.ShapeDtypeStruct((n_slots,), jnp.int32),
        ],
        in_specs=[pl.BlockSpec(memory_space=pltpu.SMEM), hbm, hbm, hbm, hbm],
        out_specs=[hbm, hbm, hbm, hbm, pl.BlockSpec(memory_space=pltpu.SMEM)],
        scratch_shapes=scratch,
        compiler_params=pltpu.CompilerParams(collective_id=0, has_side_effects=True, vmem_limit_bytes=63 << 20),
        name="attend_exchange",
    )(table, queries, enc_store, weight, cotangent)


def last_kernel(
    scale, pick_ref, back_hbm, g_hbm, att_in, dq_in, store_hbm, grad_hbm, att_out, dq_out,
    back_ref, acc_ref, store_ref, g_ref, grad_ref, att_ref, dq_ref,
    back_sem, g_sem, in_sem, out_sem,
):
    n_slots = pick_ref.shape[0]
    blk_dev, _, rows, width = acc_ref.shape
    parts = in_sem.shape[1]
    share = att_ref.shape[0] // parts

    def slot_copy(i):
        return pltpu.make_async_copy(back_hbm.at[:, i], back_ref.at[i], back_sem.at[i])

    def each_filled(body):
        def step(i, carry):
            @pl.when(pick_ref[i] >= 0)
            def _():
                body(i)
            return carry

        lax.fori_loop(0, n_slots, step, 0)

    g_copy = pltpu.make_async_copy(g_hbm, g_ref, g_sem)
    g_copy.start()
    each_filled(lambda i: slot_copy(i).start())
    ins, outs = [], []
    for part in range(parts):
        rng = pl.ds(part * share, share)
        for k, (src, buf, dst) in enumerate(((att_in, att_ref, att_out), (dq_in, dq_ref, dq_out))):
            copy = pltpu.make_async_copy(src.at[rng], buf.at[rng], in_sem.at[k, part])
            copy.start()
            ins.append((copy, pltpu.make_async_copy(buf.at[rng], dst.at[rng], out_sem.at[k, part])))
    acc_ref[...] = jnp.zeros_like(acc_ref)
    g_copy.wait()
    cols = g_ref.shape[2]
    for half in range(NC):
        for chip in range(NZ * NY):
            grad_ref[:, half, chip * cols:(chip + 1) * cols] = g_ref[half * NZ * NY + chip].astype(f32) * scale
    copy = pltpu.make_async_copy(grad_ref, grad_hbm, out_sem.at[2, 0])
    copy.start()
    outs.append(copy)

    def add(i):
        slot_copy(i).wait()
        acc_ref[pick_ref[i]] += back_ref[i].astype(f32)

    each_filled(add)
    for copy, out in ins:
        copy.wait()
        out.start()
        outs.append(out)
    some = blk_dev // parts
    for part in range(parts):
        rng = pl.ds(part * some, some)
        store_ref[rng] = acc_ref[rng].astype(bf16).reshape(some, BLOCK, width)
        copy = pltpu.make_async_copy(store_ref.at[rng], store_hbm.at[rng], out_sem.at[3, part])
        copy.start()
        outs.append(copy)
    for copy in outs:
        copy.wait()


def last_call(picks, back, grads, attended, d_queries, store_shape, w_rows, hq):
    blk_dev, _, enc_width = store_shape
    tokens = attended.shape[0]
    n_slots = back.shape[1]
    parts = 4
    hbm = pl.BlockSpec(memory_space=pl.ANY)
    vm, sem = pltpu.VMEM, pltpu.SemaphoreType.DMA
    scale = float(tokens // WIN * NEIGH * BLOCK * N_DP * N_FSDP) ** (-0.5)
    return pl.pallas_call(
        functools.partial(last_kernel, scale),
        out_shape=[
            jax.ShapeDtypeStruct(store_shape, bf16),
            jax.ShapeDtypeStruct((w_rows, NC, hq), f32),
            jax.ShapeDtypeStruct(attended.shape, bf16),
            jax.ShapeDtypeStruct(d_queries.shape, bf16),
        ],
        in_specs=[pl.BlockSpec(memory_space=pltpu.SMEM), hbm, hbm, hbm, hbm],
        out_specs=[hbm, hbm, hbm, hbm],
        scratch_shapes=[
            vm((n_slots, PHASES, ROWS, enc_width), bf16), vm((blk_dev, PHASES, ROWS, enc_width), f32),
            vm(store_shape, bf16), vm(grads.shape, bf16), vm((w_rows, NC, hq), f32),
            vm(attended.shape, bf16), vm(attended.shape, bf16),
            sem((n_slots,)), sem(()), sem((2, parts)), sem((4, parts)),
        ],
        compiler_params=pltpu.CompilerParams(vmem_limit_bytes=62 << 20),
        name="store_gradient",
    )(picks, back, grads, attended, d_queries)


def shards(queries, enc_store, kv_weight, table, cotangent):
    w_rows, _, hq = kv_weight.shape
    attended, d_queries, back, grads, picks = main_call(table.T, queries, enc_store, kv_weight, cotangent)
    d_store, grad_kv, attended, d_queries = last_call(
        picks, back, grads, attended, d_queries, enc_store.shape, w_rows, hq
    )
    return attended, d_queries, d_store, grad_kv


def solution(mesh):
    in_specs = (
        P(("dp", "fsdp"), None),
        P(("dp", "fsdp"), None, None),
        P("fsdp", None, None),
        P(),
        P(("dp", "fsdp"), None),
    )
    out_specs = (
        P(("dp", "fsdp"), None),
        P(("dp", "fsdp"), None),
        P(("dp", "fsdp"), None, None),
        P("fsdp", None, None),
    )
    return jax.shard_map(shards, mesh=mesh, in_specs=in_specs, out_specs=out_specs, check_vma=False)
```

```python
import functools

import jax
import jax.numpy as jnp
from jax import lax
from jax.experimental import pallas as pl
from jax.experimental.pallas import tpu as pltpu
from jax.sharding import PartitionSpec as P

HEAD = 128
WIN = 64
BLOCK = 128
NEIGH = 2
CAP = 2
NZ, NY, NC = 4, 2, 2
NYH, NX = 2, 4
N_DP, N_FSDP = NZ * NY * NC, NYH * NX
PHASE_ROWS = (48, 32, 32, 16)
PHASE_START = (0, 48, 80, 112)
PHASES = len(PHASE_ROWS)
SCALE = HEAD ** (-0.5)
LOG2E = 1.4426950408889634
MESH = pl.DeviceIdType.MESH
f32, bf16 = jnp.float32, jnp.bfloat16
ORDER = (
    (2, 1, 0), (2, 1, 1), (2, 0, 0), (2, 0, 1),
    (1, 1, 0), (3, 1, 0), (1, 1, 1), (3, 1, 1),
    (1, 0, 0), (3, 0, 0), (1, 0, 1), (3, 0, 1),
    (0, 1, 0), (0, 1, 1), (0, 0, 1),
)
STEPS = (2, 1, 3, 0)


def mm(a, b):
    return jnp.dot(a, b, preferred_element_type=f32)


def mm_nt(a, b):
    return lax.dot_general(a, b, (((1,), (1,)), ((), ())), preferred_element_type=f32)


def mm_tn(a, b):
    return lax.dot_general(a, b, (((0,), (0,)), ((), ())), preferred_element_type=f32)


def place():
    dp = lax.axis_index("dp")
    fs = lax.axis_index("fsdp")
    return dp, fs, dp // (NY * NC), (dp // NC) % NY, dp % NC, fs // NX, fs % NX


def two_heads(rows):
    lane = lax.broadcasted_iota(jnp.int32, rows.shape, 1)
    zero = jnp.zeros_like(rows)
    return jnp.concatenate([jnp.where(lane < HEAD, rows, zero), jnp.where(lane < HEAD, zero, rows)], axis=0)


def own_halves(full):
    return jnp.concatenate([full[:WIN, :HEAD], full[WIN:, HEAD:]], axis=1)


def pair_first(loaded):
    query, cot, keys, values = loaded
    query2, cot2 = two_heads(query), two_heads(cot)
    return query2, cot2, mm_nt(keys, query2), mm_nt(values, cot2)


def pair_softmax(first):
    query2, cot2, scores, d_probs = first
    expo = jnp.exp2((scores - jnp.max(scores, axis=0, keepdims=True)) * (SCALE * LOG2E))
    probs = expo * (1.0 / jnp.sum(expo, axis=0, keepdims=True))
    inner = jnp.sum(d_probs * probs, axis=0, keepdims=True)
    d_scores = ((probs * SCALE) * (d_probs - inner)).astype(bf16)
    return query2, cot2, probs.astype(bf16), d_scores


def pair_last(second):
    query2, cot2, probs_b, d_scores = second
    return probs_b, d_scores, mm(d_scores, query2).astype(bf16), mm(probs_b, cot2).astype(bf16)


def window_slices(win, width):
    row = pl.ds(pl.multiple_of(win * WIN, WIN), WIN)
    blk = pl.ds(win * NEIGH, NEIGH)

    def cols(pair, base):
        return pl.ds(base + pair * 2 * HEAD, 2 * HEAD)

    return row, blk, cols, width // (2 * HEAD)


def attend(wins, q_ref, c_ref, kv_ref, dkv_ref, probs_ref, ds_ref):
    width = q_ref.shape[1]
    keys_of = NEIGH * BLOCK
    items, loaded = [], []
    for win in wins:
        row, blk, cols, pairs = window_slices(win, width)
        for i in range(pairs):
            items.append((win, blk, i, cols(i, 0), cols(i, width)))
            loaded.append(
                (
                    q_ref[row, cols(i, 0)],
                    c_ref[row, cols(i, 0)],
                    kv_ref[blk, :, cols(i, 0)].reshape(keys_of, 2 * HEAD),
                    kv_ref[blk, :, cols(i, width)].reshape(keys_of, 2 * HEAD),
                )
            )
    count = len(items)
    ahead = 2
    first = [pair_first(loaded[i]) for i in range(ahead)]
    second, last = [], []
    for i in range(count):
        second.append(pair_softmax(first[i]))
        if i + ahead < count:
            first.append(pair_first(loaded[i + ahead]))
        if i >= 1:
            last.append(pair_last(second[i - 1]))
    last.append(pair_last(second[-1]))
    for (win, blk, i, key_cols, value_cols), (probs_b, d_scores, d_key, d_value) in zip(items, last):
        probs_ref[win, i] = probs_b
        ds_ref[win, i] = d_scores
        dkv_ref[blk, :, key_cols] = d_key.reshape(NEIGH, BLOCK, 2 * HEAD)
        dkv_ref[blk, :, value_cols] = d_value.reshape(NEIGH, BLOCK, 2 * HEAD)


def attend_outputs(win, kv_ref, probs_ref, ds_ref, att_ref, dq_ref):
    width = att_ref.shape[1]
    row, blk, cols, pairs = window_slices(win, width)
    keys_of = NEIGH * BLOCK
    outs = []
    for i in range(pairs):
        keys = kv_ref[blk, :, cols(i, 0)].reshape(keys_of, 2 * HEAD)
        values = kv_ref[blk, :, cols(i, width)].reshape(keys_of, 2 * HEAD)
        outs.append((own_halves(mm_tn(probs_ref[win, i], values)), own_halves(mm_tn(ds_ref[win, i], keys))))
    for i, (att, d_query) in enumerate(outs):
        att_ref[row, cols(i, 0)] = att.astype(bf16)
        dq_ref[row, cols(i, 0)] = d_query.astype(bf16)


def first_two(table_ref, device, n_req, source, blk_dev, by_request):
    first, second = jnp.int32(-1), jnp.int32(-1)
    owned = blk_dev * N_FSDP
    for r in reversed(range(n_req)):
        entry = table_ref[r % NEIGH, device * (n_req // NEIGH) + r // NEIGH]
        hit = lax.div(entry, owned) == source
        value = jnp.int32(r) if by_request else lax.rem(entry, blk_dev)
        second = jnp.where(hit, first, second)
        first = jnp.where(hit, value, first)
    return first, second


def main_kernel(
    table_ref, q_hbm, store_hbm, w_hbm, c_hbm,
    att_hbm, dq_hbm, back_hbm, grad_hbm, pick_ref,
    q_ref, c_ref, store_ref, w_raw, w_ref,
    send0, send1, send2, send3, recv0, recv1, recv2, recv3,
    kv_ref, dkv_ref, probs_ref, dsc_ref, enc_ref, enc_t_ref, dn_ref,
    gs_ref, gr_ref, rs_ref, ds_ref, dr_ref, ag_ref,
    slot_ref, inv_ref,
    in_sem, out_sem, a_send, a_recv, w_send, w_recv, ws_send, ws_recv,
    b_send, b_recv, g_send, g_recv, r_send, r_recv, d_send, d_recv, o_send, o_recv, s_send, s_recv,
):
    sends = (send0, send1, send2, send3)
    recvs = (recv0, recv1, recv2, recv3)
    dp, fs, z, yl, core, yh, x = place()
    blk_dev = store_ref.shape[0]
    n_req = kv_ref.shape[0]
    hq = q_ref.shape[1]
    enc_width = store_ref.shape[2]
    w_rows = w_hbm.shape[0]
    w_half = w_rows // NC
    grad_cols = hq // NZ
    sib = (core + 1) % NC

    def dp_dev(dz, dy, dc):
        return (((z + dz) % NZ) * (NY * NC) + ((yl + dy) % NY) * NC + (core + dc) % NC, fs)

    def fs_dev(dyh, dx):
        ylo = (yl + dyh) % NY
        return (z * (NY * NC) + ylo * NC + core, ((yh + dyh) % NYH) * NX + (x + dx) % NX)

    FS = [(dyh, dx) for dyh in range(NYH) for dx in range(NX) if (dyh, dx) != (0, 0)]

    def remote(src, dst, ssem, rsem, dev):
        return pltpu.make_async_remote_copy(
            src_ref=src, dst_ref=dst, send_sem=ssem, recv_sem=rsem, device_id=dev, device_id_type=MESH
        )

    def rows_of(p):
        return pl.ds(PHASE_START[p], PHASE_ROWS[p])

    store_loads = [
        pltpu.make_async_copy(store_hbm.at[:, rows_of(p)], store_ref.at[:, rows_of(p)], in_sem.at[3 + p])
        for p in range(PHASES)
    ]
    loads = [
        pltpu.make_async_copy(w_hbm, w_raw, in_sem.at[0]),
        pltpu.make_async_copy(q_hbm, q_ref, in_sem.at[1]),
        pltpu.make_async_copy(c_hbm, c_ref, in_sem.at[2]),
    ]
    for copy in store_loads + loads:
        copy.start()
    barrier = pltpu.get_barrier_semaphore()
    partners = [dp_dev(*o) for o in ORDER] + [fs_dev(*o) for o in FS]
    for dev in partners:
        pl.semaphore_signal(barrier, inc=1, device_id=dev, device_id_type=MESH)

    def picks(i, carry):
        dst = ((z + i // 4) % NZ) * (NY * NC) + ((yl + (i // 2) % 2) % NY) * NC + (core + i % 2) % NC
        a, b = first_two(table_ref, dst * N_FSDP + fs, n_req, dp, blk_dev, False)
        pick_ref[2 * i] = a
        pick_ref[2 * i + 1] = b
        return carry

    lax.fori_loop(0, N_DP, picks, 0)
    for copy in store_loads:
        copy.wait()
    pl.semaphore_wait(barrier, len(partners))

    a_copies, w_copies = [], []
    for p in range(PHASES):
        rows = rows_of(p)
        for dz, dy, dc in ORDER:
            i = dz * 4 + dy * 2 + dc
            for k in range(CAP):
                sends[p][2 * i + k] = store_ref[jnp.maximum(pick_ref[2 * i + k], 0), rows, :]
            slot = pl.ds(2 * i, CAP)
            copy = remote(sends[p].at[slot], recvs[p].at[slot], a_send.at[p, i], a_recv.at[p, i], dp_dev(dz, dy, dc))
            copy.start()
            a_copies.append(copy)
        for k in range(CAP):
            recvs[p][k] = store_ref[jnp.maximum(pick_ref[k], 0), rows, :]
        if p == 0:
            loads[0].wait()
            for part in range(NC):
                for kind in range(2):
                    w_ref[fs, part, :, kind * hq:(kind + 1) * hq] = w_raw[part * w_half:(part + 1) * w_half, kind, :]
            for j, (dyh, dx) in enumerate(FS):
                part = w_ref.at[fs, core]
                copy = remote(part, part, w_send.at[j], w_recv.at[j], fs_dev(dyh, dx))
                copy.start()
                w_copies.append(copy)

    mine = dp * N_FSDP + fs

    def slots(i, carry):
        src = ((z + NZ - i // 4) % NZ) * (NY * NC) + ((yl + (i // 2) % 2) % NY) * NC + (core + i % 2) % NC
        a, b = first_two(table_ref, mine, n_req, src, blk_dev, True)
        inv_ref[2 * i] = jnp.maximum(a, 0)
        inv_ref[2 * i + 1] = jnp.maximum(b, 0)
        return carry

    lax.fori_loop(0, N_DP, slots, 0)
    sources = [
        lax.div(table_ref[r % NEIGH, mine * (n_req // NEIGH) + r // NEIGH], blk_dev * N_FSDP) for r in range(n_req)
    ]
    for r in range(n_req):
        s = sources[r]
        dz = lax.rem(z + NZ - lax.div(s, NY * NC), NZ)
        dy = lax.rem(yl + lax.rem(lax.div(s, NC), NY), NY)
        index = dz * 4 + dy * 2 + lax.rem(core + lax.rem(s, NC), NC)
        seen = jnp.int32(0)
        for earlier in range(r):
            seen = seen + (sources[earlier] == s).astype(jnp.int32)
        slot_ref[r] = index * 2 + jnp.minimum(seen, CAP - 1)

    ws_copies = []
    for j, (dyh, dx) in enumerate(FS):
        w_copies[j].wait_recv()
        src_fs = ((yh + dyh) % NYH) * NX + (x + NX - dx) % NX
        part = w_ref.at[src_fs, core]
        copy = remote(part, part, ws_send.at[j], ws_recv.at[j], dp_dev(0, 0, 1))
        copy.start()
        ws_copies.append(copy)
    for copy in ws_copies:
        copy.wait_recv()

    for p in range(PHASES):
        for copy in a_copies[p * len(ORDER):(p + 1) * len(ORDER)]:
            copy.wait_recv()
        rows = rows_of(p)
        for r in range(n_req):
            enc_ref[r, rows, :] = recvs[p][slot_ref[r]]
        some = PHASE_ROWS[p]

        @pl.loop(0, kv_ref.shape[2] // 1024)
        def _(t):
            c = pl.ds(pl.multiple_of(t * 1024, 1024), 1024)
            lhs = enc_ref[:, rows, :].reshape(n_req * some, enc_width)
            out = mm(lhs, w_ref[:, :, :, c].reshape(enc_width, 1024))
            kv_ref[:, rows, c] = out.astype(bf16).reshape(n_req, some, 1024)

    loads[1].wait()
    loads[2].wait()

    together = 3

    @pl.loop(0, n_req // NEIGH // together)
    def _(step):
        attend([step * together + k for k in range(together)], q_ref, c_ref, kv_ref, dkv_ref, probs_ref, dsc_ref)

    outs = []
    for copy in a_copies:
        copy.wait_send()

    b_copies = []

    def d_neigh(p):
        rows, some = rows_of(p), PHASE_ROWS[p]
        lhs = dkv_ref[:, rows, :].reshape(n_req * some, 2 * hq)

        @pl.loop(0, 2)
        def _(t):
            part = w_ref[pl.ds(t * (N_FSDP // 2), N_FSDP // 2)].reshape(enc_width // 2, 2 * hq)
            c = pl.ds(pl.multiple_of(t * (enc_width // 2), enc_width // 2), enc_width // 2)
            dn_ref[:, :some, c] = mm_nt(lhs, part).astype(bf16).reshape(n_req, some, enc_width // 2)

        for i in range(N_DP):
            for k in range(CAP):
                sends[p][2 * i + k] = dn_ref[inv_ref[2 * i + k], :some, :]
        slot = pl.ds(0, CAP)
        copy = pltpu.make_async_copy(sends[p].at[slot], back_hbm.at[slot, rows], out_sem.at[2 + p])
        copy.start()
        outs.append(copy)

    pending = [(p, offset) for p in reversed(range(PHASES)) for offset in ORDER]

    def send_back(count):
        for _ in range(count):
            p, (dz, dy, dc) = pending[len(b_copies)]
            i = dz * 4 + dy * 2 + dc
            slot = pl.ds(2 * i, CAP)
            copy = remote(
                sends[p].at[slot], back_hbm.at[slot, rows_of(p)], b_send.at[p, i], b_recv.at[p, i],
                dp_dev((NZ - dz) % NZ, dy, dc),
            )
            copy.start()
            b_copies.append(copy)

    b_sent = []

    def wait_sent(count):
        for _ in range(count):
            b_copies[len(b_sent)].wait_send()
            b_sent.append(1)

    def grad_tile(half, t):
        tile = (z + STEPS[t]) % NZ
        c = pl.ds(pl.multiple_of(half * hq + tile * grad_cols, grad_cols), grad_cols)
        return mm(enc_t_ref[...], dkv_ref[:, :, c].reshape(n_req * BLOCK, grad_cols)).reshape(
            N_FSDP, w_rows, grad_cols
        )

    g_copies, r_copies = [], []

    def for_sibling(t):
        gs_ref[t] = grad_tile(sib, t).astype(bf16)
        copy = remote(gs_ref.at[t], gr_ref.at[t], g_send.at[t], g_recv.at[t], dp_dev(0, 0, 1))
        copy.start()
        g_copies.append(copy)

    def for_owners(t):
        own = grad_tile(core, t)
        g_copies[t].wait()
        gs_ref[t] = (own + gr_ref[t].astype(f32)).astype(bf16)
        for j, (dyh, dx) in enumerate(FS):
            dst_fs = ((yh + dyh) % NYH) * NX + (x + dx) % NX
            copy = remote(gs_ref.at[t, dst_fs], rs_ref.at[t, j], r_send.at[t, j], r_recv.at[t, j], fs_dev(dyh, dx))
            copy.start()
            r_copies.append(copy)

    part_cols = grad_cols // NY
    d_copies = []

    def reduce_tile(t):
        for copy in r_copies[t * len(FS):(t + 1) * len(FS)]:
            copy.wait_recv()
        total = gs_ref[t, fs].astype(f32)
        for j in range(len(FS)):
            total = total + rs_ref[t, j].astype(f32)
        for s in range(NY):
            ds_ref[t, s] = total[:, s * part_cols:(s + 1) * part_cols].astype(bf16)
        for dy in range(NY):
            m = len(d_copies)
            if (STEPS[t], dy) != (0, 0):
                copy = remote(
                    ds_ref.at[t, (yl + dy) % NY], dr_ref.at[m], d_send.at[m], d_recv.at[m], dp_dev(STEPS[t], dy, 0)
                )
                copy.start()
                d_copies.append(copy)

    d_neigh(3)
    send_back(15)
    d_neigh(2)
    send_back(15)
    enc_t_ref[...] = enc_ref[...].reshape(n_req * BLOCK, enc_width).T
    for_sibling(0)
    for_sibling(1)
    for_owners(0)
    for_owners(1)
    for_sibling(2)
    for_sibling(3)
    for_owners(2)
    for_owners(3)
    d_neigh(1)
    wait_sent(15)
    send_back(8)
    d_neigh(0)

    @pl.loop(0, n_req // NEIGH)
    def _(win):
        attend_outputs(win, kv_ref, probs_ref, dsc_ref, q_ref, c_ref)

    for k, (src, dst) in enumerate(((q_ref, att_hbm), (c_ref, dq_hbm))):
        copy = pltpu.make_async_copy(src, dst, out_sem.at[k])
        copy.start()
        outs.append(copy)
    reduce_tile(0)
    reduce_tile(1)
    wait_sent(15)
    send_back(7)
    reduce_tile(2)
    reduce_tile(3)
    send_back(8)

    own_chip = z * NY + yl
    chips = [(dz, dy) for dz in range(NZ) for dy in range(NY) if (dz, dy) != (0, 0)]
    total = ds_ref[STEPS.index(0), yl].astype(f32)
    for m in range(len(chips)):
        d_copies[m].wait_recv()
        total = total + dr_ref[m].astype(f32)
    ag_ref[...] = total.astype(bf16)

    def piece(chip):
        return grad_hbm.at[core * (NZ * NY) + chip]

    copy = pltpu.make_async_copy(ag_ref, piece(own_chip), out_sem.at[2 + PHASES])
    copy.start()
    outs.append(copy)
    o_copies, s_copies = [], []
    for m, (dz, dy) in enumerate(chips):
        copy = remote(ag_ref, piece(own_chip), o_send.at[m], o_recv.at[m], dp_dev(dz, dy, 0))
        copy.start()
        o_copies.append(copy)
    copy = remote(ag_ref, piece(own_chip), s_send.at[len(chips)], s_recv.at[len(chips)], dp_dev(0, 0, 1))
    copy.start()
    s_copies.append(copy)
    send_back(len(pending) - len(b_copies))
    for m, (dz, dy) in enumerate(chips):
        o_copies[m].wait_recv()
        part = piece(((z + NZ - dz) % NZ) * NY + (yl + dy) % NY)
        copy = remote(part, part, s_send.at[m], s_recv.at[m], dp_dev(0, 0, 1))
        copy.start()
        s_copies.append(copy)
    for copy in outs:
        copy.wait()
    for copy in w_copies + ws_copies + r_copies + d_copies + o_copies + b_copies[len(b_sent):]:
        copy.wait_send()
    for copy in b_copies:
        copy.wait_recv()
    for copy in s_copies:
        copy.wait()


def main_call(table, queries, enc_store, weight, cotangent):
    tokens, hq = queries.shape
    blk_dev, _, enc_width = enc_store.shape
    n_req = tokens // WIN * NEIGH
    w_rows = weight.shape[0]
    n_slots = N_DP * CAP
    n_tiles, grad_cols, pairs = NZ, hq // NZ, hq // (2 * HEAD)
    n_chips = NZ * NY
    hbm = pl.BlockSpec(memory_space=pl.ANY)
    vm = pltpu.VMEM
    sem = pltpu.SemaphoreType.DMA
    slot_refs = [vm((n_slots, rows, enc_width), bf16) for rows in PHASE_ROWS]
    scratch = [
        vm((tokens, hq), bf16), vm((tokens, hq), bf16), vm(enc_store.shape, bf16),
        vm(weight.shape, bf16), vm((N_FSDP, NC, w_rows // NC, 2 * hq), bf16),
        *slot_refs, *slot_refs,
        vm((n_req, BLOCK, 2 * hq), bf16), vm((n_req, BLOCK, 2 * hq), bf16),
        vm((n_req // NEIGH, pairs, NEIGH * BLOCK, 2 * WIN), bf16),
        vm((n_req // NEIGH, pairs, NEIGH * BLOCK, 2 * WIN), bf16), vm((n_req, BLOCK, enc_width), bf16),
        vm((enc_width, n_req * BLOCK), bf16),
        vm((n_req, max(PHASE_ROWS), enc_width), bf16),
        vm((n_tiles, N_FSDP, w_rows, grad_cols), bf16),
        vm((n_tiles, N_FSDP, w_rows, grad_cols), bf16), vm((n_tiles, N_FSDP - 1, w_rows, grad_cols), bf16),
        vm((NZ, NY, w_rows, hq // n_chips), bf16), vm((n_chips - 1, w_rows, hq // n_chips), bf16),
        vm((w_rows, hq // n_chips), bf16),
        pltpu.SMEM((n_req,), jnp.int32), pltpu.SMEM((n_slots,), jnp.int32),
        sem((3 + PHASES,)), sem((3 + PHASES,)), sem((PHASES, N_DP)), sem((PHASES, N_DP)),
        sem((N_FSDP - 1,)), sem((N_FSDP - 1,)), sem((N_FSDP - 1,)), sem((N_FSDP - 1,)),
        sem((PHASES, N_DP)), sem((PHASES, N_DP)), sem((n_tiles,)), sem((n_tiles,)),
        sem((n_tiles, N_FSDP - 1)), sem((n_tiles, N_FSDP - 1)), sem((n_chips - 1,)), sem((n_chips - 1,)),
        sem((n_chips - 1,)), sem((n_chips - 1,)), sem((n_chips,)), sem((n_chips,)),
    ]
    return pl.pallas_call(
        main_kernel,
        out_shape=[
            jax.ShapeDtypeStruct((tokens, hq), bf16),
            jax.ShapeDtypeStruct((tokens, hq), bf16),
            jax.ShapeDtypeStruct((n_slots, BLOCK, enc_width), bf16),
            jax.ShapeDtypeStruct((NC * n_chips, w_rows, hq // n_chips), bf16),
            jax.ShapeDtypeStruct((n_slots,), jnp.int32),
        ],
        in_specs=[pl.BlockSpec(memory_space=pltpu.SMEM), hbm, hbm, hbm, hbm],
        out_specs=[hbm, hbm, hbm, hbm, pl.BlockSpec(memory_space=pltpu.SMEM)],
        scratch_shapes=scratch,
        compiler_params=pltpu.CompilerParams(collective_id=0, has_side_effects=True, vmem_limit_bytes=63 << 20),
        name="attend_exchange",
    )(table, queries, enc_store, weight, cotangent)


def last_kernel(
    scale, pick_ref, back_hbm, g_hbm, att_in, dq_in, store_hbm, grad_hbm, att_out, dq_out,
    back_ref, acc_ref, store_ref, g_ref, grad_ref, att_ref, dq_ref,
    back_sem, g_sem, in_sem, out_sem,
):
    n_slots = pick_ref.shape[0]
    blk_dev = acc_ref.shape[0]
    parts = in_sem.shape[1]
    share = att_ref.shape[0] // parts

    def slot_copy(i):
        return pltpu.make_async_copy(back_hbm.at[i], back_ref.at[i], back_sem.at[i])

    def each_filled(body):
        def step(i, carry):
            @pl.when(pick_ref[i] >= 0)
            def _():
                body(i)
            return carry

        lax.fori_loop(0, n_slots, step, 0)

    g_copy = pltpu.make_async_copy(g_hbm, g_ref, g_sem)
    g_copy.start()
    each_filled(lambda i: slot_copy(i).start())
    ins, outs = [], []
    for part in range(parts):
        rng = pl.ds(part * share, share)
        for k, (src, buf, dst) in enumerate(((att_in, att_ref, att_out), (dq_in, dq_ref, dq_out))):
            copy = pltpu.make_async_copy(src.at[rng], buf.at[rng], in_sem.at[k, part])
            copy.start()
            ins.append((copy, pltpu.make_async_copy(buf.at[rng], dst.at[rng], out_sem.at[k, part])))
    acc_ref[...] = jnp.zeros_like(acc_ref)
    g_copy.wait()
    cols = g_ref.shape[2]
    for half in range(NC):
        for chip in range(NZ * NY):
            grad_ref[:, half, chip * cols:(chip + 1) * cols] = g_ref[half * NZ * NY + chip].astype(f32) * scale
    copy = pltpu.make_async_copy(grad_ref, grad_hbm, out_sem.at[2, 0])
    copy.start()
    outs.append(copy)

    def add(i):
        slot_copy(i).wait()
        acc_ref[pick_ref[i]] += back_ref[i].astype(f32)

    each_filled(add)
    for copy, out in ins:
        copy.wait()
        out.start()
        outs.append(out)
    some = blk_dev // parts
    for part in range(parts):
        rng = pl.ds(part * some, some)
        store_ref[rng] = acc_ref[rng].astype(bf16)
        copy = pltpu.make_async_copy(store_ref.at[rng], store_hbm.at[rng], out_sem.at[3, part])
        copy.start()
        outs.append(copy)
    for copy in outs:
        copy.wait()


def last_call(picks, back, grads, attended, d_queries, store_shape, w_rows, hq):
    tokens = attended.shape[0]
    parts = 4
    hbm = pl.BlockSpec(memory_space=pl.ANY)
    vm, sem = pltpu.VMEM, pltpu.SemaphoreType.DMA
    scale = float(tokens // WIN * NEIGH * BLOCK * N_DP * N_FSDP) ** (-0.5)
    return pl.pallas_call(
        functools.partial(last_kernel, scale),
        out_shape=[
            jax.ShapeDtypeStruct(store_shape, bf16),
            jax.ShapeDtypeStruct((w_rows, NC, hq), f32),
            jax.ShapeDtypeStruct(attended.shape, bf16),
            jax.ShapeDtypeStruct(d_queries.shape, bf16),
        ],
        in_specs=[pl.BlockSpec(memory_space=pltpu.SMEM), hbm, hbm, hbm, hbm],
        out_specs=[hbm, hbm, hbm, hbm],
        scratch_shapes=[
            vm(back.shape, bf16), vm(store_shape, f32),
            vm(store_shape, bf16), vm(grads.shape, bf16), vm((w_rows, NC, hq), f32),
            vm(attended.shape, bf16), vm(attended.shape, bf16),
            sem((back.shape[0],)), sem(()), sem((2, parts)), sem((4, parts)),
        ],
        compiler_params=pltpu.CompilerParams(vmem_limit_bytes=62 << 20),
        name="store_gradient",
    )(picks, back, grads, attended, d_queries)


def shards(queries, enc_store, kv_weight, table, cotangent):
    w_rows, _, hq = kv_weight.shape
    attended, d_queries, back, grads, picks = main_call(table.T, queries, enc_store, kv_weight, cotangent)
    d_store, grad_kv, attended, d_queries = last_call(
        picks, back, grads, attended, d_queries, enc_store.shape, w_rows, hq
    )
    return attended, d_queries, d_store, grad_kv


def solution(mesh):
    in_specs = (
        P(("dp", "fsdp"), None),
        P(("dp", "fsdp"), None, None),
        P("fsdp", None, None),
        P(),
        P(("dp", "fsdp"), None),
    )
    out_specs = (
        P(("dp", "fsdp"), None),
        P(("dp", "fsdp"), None),
        P(("dp", "fsdp"), None, None),
        P("fsdp", None, None),
    )
    return jax.shard_map(shards, mesh=mesh, in_specs=in_specs, out_specs=out_specs, check_vma=False)
```
